32 devices in a mesh: wide: 16 (over z, y, core), narrow: 2 (over x).
Axes of the slice: x: 2, y: 2, z: 4, core: 2. Of those that a mesh axis runs over, the one named last changes fastest.
Arguments:
- grid: bfloat16 [192, 256, 1440], P('wide', 'narrow'), may hold values from -6 to 6
- quad_weights: float32 [192], P('wide'), may hold values from 0.25 to 2
- orders: int32 [32], replicated, may hold values from 0 to 719, as said below
- legendre: bfloat16 [32, 720, 192], P('wide'), as said below
- mix_real: bfloat16 [256, 256], replicated, may hold values from -0.25 to 0.25
- mix_imag: bfloat16 [256, 256], replicated, may hold values from -0.25 to 0.25
- filter_gain: bfloat16 [720, 256], replicated, may hold values from 0.25 to 4
Outputs:
- field_out: bfloat16 [192, 256, 1440], P('wide', 'narrow')
The draws below stay inside these ranges and needn't reach their ends.
Inputs may be any that keep to these rules, and one draw needn't show every extreme that they name: `orders`: every order appears in one slot only; slots 2 q and 2 q + 1 hold p and 719 - p for some p below 360, so the 2 slots of a device come in such pairs. legendre[k, l, :] is zero for every degree l below orders[k].
All inputs are finite; a program needn't handle non-finite values.
Results may differ from the reference program's by a relative error of at most 0.007.
Values may be sent and summed in bfloat16 or wider, within the bound.
A program may use at most 64 MiB of HBM per device.

```python
import math
import jax
import jax.numpy as jnp
from jax import lax

NLON = 1440
L = 720
C = 256
LAT_DEV = 12
M = 32
NLAT = 192
N_WIDE = 16


def pair_orders(key):
    chosen = jax.random.permutation(key, L // 2)[:M // 2].astype(jnp.int32)
    position = jax.random.randint(jax.random.fold_in(key, 1), (), 0, M // 2)
    forced = chosen.at[position].set(0)
    half_pairs = jnp.where(jnp.any(chosen == 0), chosen, forced)
    return jnp.stack([half_pairs, L - 1 - half_pairs], axis=1).reshape(M)


def draw_orders(key, part):
    return pair_orders(jax.random.fold_in(key, 11))


def draw_legendre(key, part):
    order_slots = pair_orders(jax.random.fold_in(key, 11))
    value_key = jax.random.fold_in(key, 12)
    entries = jax.random.normal(value_key, (M, L, NLAT), jnp.float32)
    degree = jnp.arange(L, dtype=jnp.int32)[None, :, None]
    keep_mask = degree >= order_slots[:, None, None]
    return (jnp.where(keep_mask, entries, 0.0) * NLAT ** (-0.5)).astype(jnp.bfloat16)


def level_of(rng, dims, split, least, high):
    loudness, own = 1.0, jax.random.fold_in(rng, 6)
    for axis_at, blocks in split:
        steps = jnp.exp(jax.random.uniform(jax.random.fold_in(own, axis_at), (blocks,), jnp.float32, least / len(split), high / len(split)))
        loudness = loudness * jnp.repeat(steps, dims[axis_at] // blocks).reshape([-1 if axis == axis_at else 1 for axis in range(len(dims))])
    return loudness


def noise(stream_key, extent, width, reach, cuts=(), kind=jnp.bfloat16):
    level = level_of(stream_key, extent, cuts, -0.22, 0.18) if cuts else 1.0
    values = jax.random.normal(stream_key, extent, jnp.float32) * width * level
    return jnp.minimum(jnp.maximum(values, -reach), reach).astype(kind)


def setup_inputs(seed: int = 0) -> dict:
    keys = jax.random.split(jax.random.key(seed), 8)
    return {
        "grid": noise(keys[0], (NLAT, C, NLON), 1.0, 6.0, ((0, 16), (1, 2))),
        "quad_weights": jnp.clip(jnp.exp(math.log(2.0) - 2.0794415 * jax.random.uniform(keys[1], (NLAT,), jnp.float32) ** level_of(keys[1], (NLAT,), ((0, 16),), -0.2, 0.2)), 0.25, 2.0),
        "orders": draw_orders(jax.random.fold_in(keys[7], 71), 0),
        "legendre": draw_legendre(jax.random.fold_in(keys[7], 71), 0),
        "mix_real": noise(keys[4], (C, C), (2 * C) ** -0.5, 0.25),
        "mix_imag": noise(keys[5], (C, C), (2 * C) ** -0.5, 0.25),
        "filter_gain": jnp.clip(jnp.exp(jax.random.uniform(keys[6], (L, C), jnp.float32, math.log(0.25), math.log(4.0))), 0.25, 4.0).astype(jnp.bfloat16),
    }


highest = lax.Precision.HIGHEST

def fourier_tables(orders, lon_count):
    columns = jnp.arange(lon_count, dtype=jnp.int32)
    phase_int = orders.astype(jnp.int32)[:, None] * columns[None, :] % lon_count
    angles = phase_int.astype(jnp.float32) * (2.0 * math.pi / lon_count)
    return (jnp.cos(angles).astype(jnp.bfloat16), jnp.sin(angles).astype(jnp.bfloat16))

def reference(grid, quad_weights, orders, legendre, mix_real, mix_imag, filter_gain):
    cosine_low, sine_low = fourier_tables(orders, NLON)
    cosine_table = cosine_low.astype(jnp.float32)
    sine_table = sine_low.astype(jnp.float32)
    factor = 1.0 / math.sqrt(NLON)

    def forward(lat_block):
        lat_rows, weights = lat_block
        values = lat_rows.astype(jnp.float32)
        real_part = jnp.einsum('acn,kn->kac', values, cosine_table, precision=highest) * factor
        imag_part = -jnp.einsum('acn,kn->kac', values, sine_table, precision=highest) * factor
        spectra = jnp.stack([real_part, imag_part], axis=2) * weights[None, :, None, None]
        return spectra.astype(jnp.bfloat16)
    blocks = lax.map(forward, (grid.reshape(N_WIDE, LAT_DEV, C, NLON), quad_weights.reshape(N_WIDE, LAT_DEV)))
    spectra = jnp.transpose(blocks, (1, 0, 2, 3, 4)).reshape(M, NLAT, 2 * C)
    legendre_f = legendre.astype(jnp.float32)
    coeffs = jnp.einsum('mlx,mxk->mlk', legendre_f, spectra.astype(jnp.float32)).astype(jnp.bfloat16)
    coeffs = coeffs.reshape(M * L, 2, C)
    real_in = coeffs[:, 0]
    imag_in = coeffs[:, 1]
    mixed_real = jnp.dot(real_in, mix_real, preferred_element_type=jnp.float32) - jnp.dot(imag_in, mix_imag, preferred_element_type=jnp.float32)
    mixed_imag = jnp.dot(real_in, mix_imag, preferred_element_type=jnp.float32) + jnp.dot(imag_in, mix_real, preferred_element_type=jnp.float32)
    gain_rows = jnp.tile(filter_gain.astype(jnp.float32), (M, 1))
    mixed_coeffs = jnp.stack([mixed_real * gain_rows, mixed_imag * gain_rows], axis=1).astype(jnp.bfloat16)
    mixed_coeffs = mixed_coeffs.reshape(M, L, 2 * C)
    synthesis = jnp.einsum('mlx,mlk->mxk', legendre_f, mixed_coeffs.astype(jnp.float32)).astype(jnp.bfloat16)
    synthesis = jnp.transpose(synthesis.reshape(M, N_WIDE, LAT_DEV, 2, C), (1, 0, 2, 3, 4))

    def inverse(lat_block):
        values = lat_block.astype(jnp.float32)
        field_out = jnp.einsum('kac,kn->acn', values[:, :, 0], cosine_table, precision=highest)
        field_out = field_out - jnp.einsum('kac,kn->acn', values[:, :, 1], sine_table, precision=highest)
        return (field_out / math.sqrt(M)).astype(jnp.bfloat16)
    result = lax.map(inverse, synthesis)
    return result.reshape(NLAT, C, NLON)
```

```python
import functools
import math

import jax
import jax.numpy as jnp
from jax import lax
from jax.experimental import pallas as pl
from jax.experimental.pallas import tpu as pltpu
from jax.sharding import PartitionSpec as P

MESH = pl.DeviceIdType.MESH
SUB = 8
LANES = 128


def fourier_tables(orders, lon_count):
    columns = jnp.arange(lon_count, dtype=jnp.int32)
    phase_int = orders[:, None] * columns[None, :] % lon_count
    angles = phase_int.astype(jnp.float32) * (2.0 * math.pi / lon_count)
    return (jnp.cos(angles).astype(jnp.bfloat16), jnp.sin(angles).astype(jnp.bfloat16))


def general_shards(grid, quad_weights, orders, legendre, mix_real, mix_imag, filter_gain):
    lon_count = grid.shape[2]
    order_count = orders.shape[0]
    cosine_table, sine_table = fourier_tables(orders, lon_count)
    factor = 1.0 / math.sqrt(lon_count)
    real_part = (
        jnp.einsum("acn,kn->kac", grid, cosine_table, preferred_element_type=jnp.float32) * factor
    )
    imag_part = (
        -jnp.einsum("acn,kn->kac", grid, sine_table, preferred_element_type=jnp.float32) * factor
    )
    spectra = (
        jnp.stack([real_part, imag_part], axis=2) * quad_weights[None, :, None, None]
    ).astype(jnp.bfloat16)
    by_order = lax.all_to_all(spectra, "wide", split_axis=0, concat_axis=1, tiled=True)
    m_dev = by_order.shape[0]
    lat_count = by_order.shape[1]
    chan_dev = by_order.shape[3]
    deg_count = legendre.shape[1]
    coeffs = jnp.einsum(
        "mlx,mxk->mlk",
        legendre,
        by_order.reshape(m_dev, lat_count, 2 * chan_dev),
        preferred_element_type=jnp.float32,
    )
    coeffs = coeffs.astype(jnp.bfloat16).reshape(m_dev, deg_count, 2, chan_dev)
    deg_dev = deg_count // lax.axis_size("narrow")
    gain_rows = lax.dynamic_slice_in_dim(
        filter_gain, lax.axis_index("narrow") * deg_dev, deg_dev, 0
    ).astype(jnp.float32)
    upper = jnp.concatenate([mix_real, mix_imag], axis=1)
    lower = jnp.concatenate([-mix_imag, mix_real], axis=1)
    wide_block = jnp.concatenate([upper, lower], axis=0)
    fragment = lax.all_to_all(coeffs, "narrow", split_axis=1, concat_axis=3, tiled=True)
    frag_count = fragment.shape[0]
    chan_all = fragment.shape[3]
    flat_rows = fragment.reshape(frag_count * deg_dev, 2 * chan_all)
    product = jnp.dot(flat_rows, wide_block, preferred_element_type=jnp.float32)
    product = product.reshape(frag_count, deg_dev, 2, chan_all) * gain_rows[None, :, None, :]
    mixed_coeffs = product.astype(jnp.bfloat16)
    back_coeffs = lax.all_to_all(mixed_coeffs, "narrow", split_axis=3, concat_axis=1, tiled=True)
    synthesis = jnp.einsum(
        "mlx,mlk->mxk",
        legendre,
        back_coeffs.reshape(m_dev, deg_count, 2 * chan_dev),
        preferred_element_type=jnp.float32,
    )
    synthesis = synthesis.astype(jnp.bfloat16).reshape(m_dev, lat_count, 2, chan_dev)
    by_latitude = lax.all_to_all(synthesis, "wide", split_axis=1, concat_axis=0, tiled=True)
    field_out = jnp.einsum(
        "kac,kn->acn", by_latitude[:, :, 0], cosine_table, preferred_element_type=jnp.float32
    )
    field_out = field_out - jnp.einsum(
        "kac,kn->acn", by_latitude[:, :, 1], sine_table, preferred_element_type=jnp.float32
    )
    return (field_out / math.sqrt(order_count)).astype(jnp.bfloat16)


def turn_cosine(phase, period):
    quarter = period // 4
    turns = jnp.floor(phase * (1.0 / quarter) + 0.5)
    angle = (phase - turns * quarter) * (2.0 * math.pi / period)
    quadrant = turns - 4.0 * jnp.floor(turns * 0.25)
    sq = angle * angle
    cosine = 1.0 + sq * (-0.5 + sq * (1.0 / 24 + sq * (-1.0 / 720 + sq * (1.0 / 40320))))
    sine = angle * (1.0 + sq * (-1.0 / 6 + sq * (1.0 / 120 + sq * (-1.0 / 5040 + sq * (1.0 / 362880)))))
    odd = (quadrant == 1.0) | (quadrant == 3.0)
    flip = (quadrant == 1.0) | (quadrant == 2.0)
    value = jnp.where(odd, sine, cosine)
    return jnp.where(flip, -value, value)


def spectral_kernel(
    dims, orders_hbm, quad_hbm, grid_hbm, leg_hbm, mixr_hbm, mixi_hbm, gain_hbm,
    out_ref, tabt_ref,
    grid_v, leg_v, mixr_v, mixi_v, gain_v, tab, spread, send1, recv1, lt, lf,
    weight, mixed, send2, recv2, flat2, orders_ref, quad_ref,
    grid_sem, in_sem, local_sem, s_send, s_recv, b_send, b_recv,
):
    n_wide, lat_dev, lon_count, chan, m_dev, deg_count = dims
    order_count = n_wide * m_dev
    rows = 2 * order_count
    rest = lat_dev - SUB
    half = n_wide * SUB
    pairs = lat_dev // 2
    others = m_dev * n_wide - 1
    me = lax.axis_index("wide")
    x = lax.axis_index("narrow")

    scalar_copies = []
    for i, (src, dst) in enumerate(((orders_hbm, orders_ref), (quad_hbm, quad_ref))):
        copy = pltpu.make_async_copy(src, dst, in_sem.at[4 + i])
        copy.start()
        scalar_copies.append(copy)
    grid_copies = []
    for p in range(pairs):
        copy = pltpu.make_async_copy(
            grid_hbm.at[pl.ds(2 * p, 2)], grid_v.at[pl.ds(2 * p, 2)], grid_sem.at[p]
        )
        copy.start()
        grid_copies.append(copy)
    in_copies = []
    for i, (src, dst) in enumerate(
        ((leg_hbm.at[x], leg_v), (mixr_hbm, mixr_v), (mixi_hbm, mixi_v), (gain_hbm, gain_v))
    ):
        copy = pltpu.make_async_copy(src, dst, in_sem.at[i])
        copy.start()
        in_copies.append(copy)

    steps = []
    bit = 1
    while bit < n_wide:
        steps.append(bit * (1 - 2 * (me // bit % 2)))
        bit *= 2

    def flipped(d):
        return me + functools.reduce(
            lambda a, b: a + b, [s for i, s in enumerate(steps) if d >> i & 1], 0
        )

    peers = []
    for d in reversed(range(n_wide)):
        for dx in (1, 0):
            if d or dx:
                peers.append((flipped(d), 1 - x if dx else x))

    barrier = pltpu.get_barrier_semaphore()
    for to in peers:
        pl.semaphore_signal(barrier, inc=1, device_id=to, device_id_type=MESH)

    for copy in scalar_copies:
        copy.wait()
    row = lax.broadcasted_iota(jnp.int32, (rows, LANES), 0)
    lane = lax.broadcasted_iota(jnp.int32, (rows, LANES), 1)
    block_rows = 2 * n_wide
    order_row = jnp.zeros((rows, LANES), jnp.int32)
    for j in range(m_dev):
        for w in range(n_wide):
            slot = orders_ref[w * m_dev + j]
            hit = (row == j * block_rows + w) | (row == j * block_rows + n_wide + w)
            order_row = jnp.where(hit, slot, order_row)
    shift = jnp.zeros((rows, LANES), jnp.int32)
    for j in range(m_dev):
        low = j * block_rows + n_wide
        shift = jnp.where((row >= low) & (row < low + n_wide), lon_count // 4, shift)
    for start in range(0, lon_count, LANES):
        size = min(LANES, lon_count - start)
        phase = (order_row * (lane + start) + shift).astype(jnp.float32)
        value = turn_cosine(phase, lon_count)
        tab[:, start:start + size] = value.astype(jnp.bfloat16)[:, :size]
        tabt_ref[start:start + size, :] = jnp.transpose(value)[:size].astype(jnp.bfloat16)

    factor = 1.0 / math.sqrt(lon_count)

    def transform(p):
        grid_copies[p].wait()
        rhs = jnp.concatenate([grid_v[2 * p], grid_v[2 * p + 1]], axis=1)
        res = jnp.dot(tab[...], rhs, preferred_element_type=jnp.float32)
        for i in range(2):
            a = 2 * p + i
            spread[a * rows:(a + 1) * rows, :] = res[:, i * chan:(i + 1) * chan] * (
                quad_ref[a] * factor
            )

    def row_of(j, ri, w):
        return j * block_rows + ri * n_wide + w

    heads, tails = pl.ds(0, 2), pl.ds(2, 1)

    def out_copy(part, to):
        where = tails if part else heads
        return pltpu.make_async_remote_copy(
            src_ref=send1.at[to[1] * n_wide + to[0], where],
            dst_ref=recv1.at[x * n_wide + me, where],
            send_sem=s_send.at[part],
            recv_sem=s_recv.at[part],
            device_id=to,
            device_id_type=MESH,
        )

    def own_copy(part):
        where = tails if part else heads
        mine = x * n_wide + me
        return pltpu.make_async_copy(
            send1.at[mine, where], recv1.at[mine, where], local_sem.at[part]
        )

    for p in range(SUB // 2):
        transform(p)
    for j in range(m_dev):
        for w in range(n_wide):
            for ri in range(2):
                send1[j * n_wide + w, ri] = spread[
                    pl.ds(row_of(j, ri, w), SUB, stride=rows), :
                ].astype(jnp.bfloat16)
    pl.semaphore_wait(barrier, others)
    for to in peers:
        out_copy(0, to).start()
    own_copy(0).start()

    for p in range(SUB // 2, pairs):
        transform(p)
    for j in range(m_dev):
        for w in range(n_wide):
            both = [
                spread[pl.ds(SUB * rows + row_of(j, ri, w), rest, stride=rows), :]
                for ri in range(2)
            ]
            send1[j * n_wide + w, 2] = jnp.concatenate(both, axis=0).astype(jnp.bfloat16)
    for to in peers:
        out_copy(1, to).start()
    own_copy(1).start()

    for copy in in_copies:
        copy.wait()
    lat_count = n_wide * lat_dev
    slot = lax.broadcasted_iota(jnp.int32, (2 * half, lat_count), 0)
    lat = lax.broadcasted_iota(jnp.int32, (2 * half, lat_count), 1)
    local = slot % SUB
    device = jnp.where(slot < half, slot, slot - half) // SUB
    want = device * lat_dev + jnp.where(slot < half, local, SUB + local % rest)
    pick = (want == lat).astype(jnp.bfloat16)
    moved = jnp.dot(pick, leg_v[...], preferred_element_type=jnp.float32)
    lt[...] = moved.astype(jnp.bfloat16)
    lf[...] = jnp.transpose(moved).astype(jnp.bfloat16)
    for i in range(m_dev):
        for o in range(m_dev):
            re = mixr_v[i * chan:(i + 1) * chan, o * chan:(o + 1) * chan]
            im = mixi_v[i * chan:(i + 1) * chan, o * chan:(o + 1) * chan]
            top, left = 2 * i * chan, 2 * o * chan
            weight[top:top + chan, left:left + chan] = re
            weight[top:top + chan, left + chan:left + 2 * chan] = im
            weight[top + chan:top + 2 * chan, left:left + chan] = -im
            weight[top + chan:top + 2 * chan, left + chan:left + 2 * chan] = re

    def all_arrived(buf, where, sem):
        piece = buf.at[pl.ds(0, others), where]
        pltpu.make_async_copy(piece, piece, sem).wait()

    for part, where in enumerate((heads, tails)):
        own_copy(part).wait()
        all_arrived(recv1, where, s_recv.at[part])

    tail_row = lax.broadcasted_iota(jnp.int32, (half, chan), 0) % SUB
    upper = tail_row < rest
    columns = []
    for i in range(m_dev):
        mine = pl.ds(i * n_wide, n_wide)
        tail = recv1[mine, 2].reshape(half, chan)
        for ri in range(2):
            head = recv1[mine, ri].reshape(half, chan)
            keep = upper if ri == 0 else jnp.logical_not(upper)
            columns.append(
                jnp.concatenate([head, jnp.where(keep, tail, jnp.zeros_like(tail))], axis=0)
            )
    spec = jnp.concatenate(columns, axis=1)
    coeffs = jnp.dot(lf[...], spec, preferred_element_type=jnp.float32).astype(jnp.bfloat16)

    def back_copy(to):
        return pltpu.make_async_remote_copy(
            src_ref=send2.at[to[1] * n_wide + to[0]],
            dst_ref=recv2.at[x * n_wide + me],
            send_sem=b_send,
            recv_sem=b_recv,
            device_id=to,
            device_id_type=MESH,
        )

    for o in range(m_dev):
        cols = pl.ds(2 * o * chan, 2 * chan)
        product = jnp.dot(coeffs, weight[:, cols], preferred_element_type=jnp.float32)
        gain = gain_v[:, o * chan:(o + 1) * chan].astype(jnp.float32)
        gain = jnp.concatenate([gain, gain], axis=1)
        mixed[o] = (product * gain).astype(jnp.bfloat16)
        syn = jnp.dot(lt[...], mixed[o], preferred_element_type=jnp.float32)
        re, im = syn[:, :chan], syn[:, chan:]
        mine = pl.ds(o * n_wide, n_wide)
        tail = jnp.where(upper, re[half:], im[half:])
        for t, tile in enumerate((re[:half], im[:half], tail)):
            send2[mine, t] = tile.astype(jnp.bfloat16).reshape(n_wide, SUB, chan)

    for to in peers:
        back_copy(to).start()
    mine = x * n_wide + me
    own_back = pltpu.make_async_copy(send2.at[mine], recv2.at[mine], local_sem.at[2])
    own_back.start()
    for part, where in enumerate((heads, tails)):
        all_arrived(send1, where, s_send.at[part])
    own_back.wait()
    everything = pl.ds(0, 3)
    all_arrived(recv2, everything, b_recv)
    flat2[...] = recv2[...].astype(jnp.float32).reshape(rows * 3 * SUB // 2, chan)
    for a in range(lat_dev):
        for j in range(m_dev):
            for ri in range(2):
                at = ri * SUB + a if a < SUB else 2 * SUB + ri * rest + a - SUB
                top = row_of(j, ri, 0)
                out_ref[a, top:top + n_wide, :] = flat2[
                    pl.ds(j * n_wide * 3 * SUB + at, n_wide, stride=3 * SUB), :
                ].astype(jnp.bfloat16)
    all_arrived(send2, everything, b_send)


def field_kernel(scale, tabt_ref, syn_ref, out_hbm, held, sem):
    lat_dev, _, chan = held.shape
    copies = []
    for p in range(lat_dev // 2):
        rhs = jnp.concatenate([syn_ref[2 * p], syn_ref[2 * p + 1]], axis=1)
        res = jnp.dot(tabt_ref[...], rhs, preferred_element_type=jnp.float32) * scale
        res = res.astype(jnp.bfloat16)
        held[2 * p] = res[:, :chan]
        held[2 * p + 1] = res[:, chan:]
        both = pl.ds(2 * p, 2)
        copy = pltpu.make_async_copy(held.at[both], out_hbm.at[both], sem.at[p])
        copy.start()
        copies.append(copy)
    for copy in copies:
        copy.wait()


def fast_shards(grid, quad_weights, orders, legendre, mix_real, mix_imag, filter_gain):
    lat_dev, chan, lon_count = grid.shape
    order_count = orders.shape[0]
    m_dev, deg_count, lat_count = legendre.shape
    n_wide = lax.axis_size("wide")
    rows = 2 * order_count
    half = n_wide * SUB
    bf16, f32 = jnp.bfloat16, jnp.float32
    vmem = pl.BlockSpec(memory_space=pltpu.VMEM)
    hbm = pl.BlockSpec(memory_space=pltpu.HBM)
    dims = (n_wide, lat_dev, lon_count, chan, m_dev, deg_count)
    chan_all = mix_real.shape[0]
    dma = pltpu.SemaphoreType.DMA
    synthesis, table = pl.pallas_call(
        functools.partial(spectral_kernel, dims),
        out_shape=(
            jax.ShapeDtypeStruct((lat_dev, rows, chan), bf16),
            jax.ShapeDtypeStruct((lon_count, rows), bf16),
        ),
        in_specs=[hbm] * 7,
        out_specs=(vmem, vmem),
        scratch_shapes=[
            pltpu.VMEM((lat_dev, lon_count, chan), bf16),
            pltpu.VMEM((lat_count, deg_count), bf16),
            pltpu.VMEM((chan_all, chan_all), bf16),
            pltpu.VMEM((chan_all, chan_all), bf16),
            pltpu.VMEM((deg_count, chan_all), bf16),
            pltpu.VMEM((rows, lon_count), bf16),
            pltpu.VMEM((lat_dev * rows, chan), f32),
            pltpu.VMEM((order_count, 3, SUB, chan), bf16),
            pltpu.VMEM((order_count, 3, SUB, chan), bf16),
            pltpu.VMEM((2 * half, deg_count), bf16),
            pltpu.VMEM((deg_count, 2 * half), bf16),
            pltpu.VMEM((4 * chan, 4 * chan), bf16),
            pltpu.VMEM((m_dev, deg_count, 2 * chan), bf16),
            pltpu.VMEM((order_count, 3, SUB, chan), bf16),
            pltpu.VMEM((order_count, 3, SUB, chan), bf16),
            pltpu.VMEM((order_count * 3 * SUB, chan), f32),
            pltpu.SMEM((order_count,), jnp.int32),
            pltpu.SMEM((lat_dev,), f32),
            dma((lat_dev // 2,)),
            dma((6,)),
            dma((3,)),
            dma((2,)),
            dma((2,)),
            dma,
            dma,
        ],
        compiler_params=pltpu.CompilerParams(
            collective_id=0, has_side_effects=True, vmem_limit_bytes=40 * 2**20
        ),
        name="spectral",
    )(*(pltpu.with_memory_space_constraint(v, pltpu.HBM) for v in (
        orders, quad_weights, jnp.transpose(grid, (0, 2, 1)), jnp.transpose(legendre, (0, 2, 1)),
        mix_real, mix_imag, filter_gain,
    )))
    field = pl.pallas_call(
        functools.partial(field_kernel, 1.0 / math.sqrt(order_count)),
        out_shape=jax.ShapeDtypeStruct((lat_dev, lon_count, chan), bf16),
        in_specs=[vmem, vmem],
        out_specs=pl.BlockSpec(memory_space=pl.ANY),
        scratch_shapes=[pltpu.VMEM((lat_dev, lon_count, chan), bf16), dma((lat_dev // 2,))],
        compiler_params=pltpu.CompilerParams(vmem_limit_bytes=24 * 2**20),
        name="field",
    )(table, synthesis)
    return jnp.transpose(field, (0, 2, 1))


def shards(grid, quad_weights, orders, legendre, mix_real, mix_imag, filter_gain):
    lat_dev, chan, lon_count = grid.shape
    m_dev = legendre.shape[0]
    n_wide = lax.axis_size("wide")
    rest = lat_dev - SUB
    fits = (
        lax.axis_size("narrow") == 2
        and chan == LANES
        and lon_count % 4 == 0
        and m_dev == 2
        and 2 * rest == SUB
        and lat_dev % 2 == 0
        and n_wide % 16 == 0
        and n_wide & (n_wide - 1) == 0
        and lon_count * lon_count < 2**24
    )
    body = fast_shards if fits else general_shards
    return body(grid, quad_weights, orders, legendre, mix_real, mix_imag, filter_gain)


def solution(mesh):
    placed = (P("wide", "narrow", None), P("wide"), P(), P("wide", None, None), P(), P(), P())
    return jax.shard_map(
        shards, mesh=mesh, in_specs=placed, out_specs=P("wide", "narrow", None), check_vma=False
    )
```

```python
import functools
import math

import jax
import jax.numpy as jnp
from jax import lax
from jax.experimental import pallas as pl
from jax.experimental.pallas import tpu as pltpu
from jax.sharding import PartitionSpec as P

MESH = pl.DeviceIdType.MESH
SUB = 8
LANES = 128


def fourier_tables(orders, lon_count):
    columns = jnp.arange(lon_count, dtype=jnp.int32)
    phase_int = orders[:, None] * columns[None, :] % lon_count
    angles = phase_int.astype(jnp.float32) * (2.0 * math.pi / lon_count)
    return (jnp.cos(angles).astype(jnp.bfloat16), jnp.sin(angles).astype(jnp.bfloat16))


def general_shards(grid, quad_weights, orders, legendre, mix_real, mix_imag, filter_gain):
    lon_count = grid.shape[2]
    order_count = orders.shape[0]
    cosine_table, sine_table = fourier_tables(orders, lon_count)
    factor = 1.0 / math.sqrt(lon_count)
    real_part = (
        jnp.einsum("acn,kn->kac", grid, cosine_table, preferred_element_type=jnp.float32) * factor
    )
    imag_part = (
        -jnp.einsum("acn,kn->kac", grid, sine_table, preferred_element_type=jnp.float32) * factor
    )
    spectra = (
        jnp.stack([real_part, imag_part], axis=2) * quad_weights[None, :, None, None]
    ).astype(jnp.bfloat16)
    by_order = lax.all_to_all(spectra, "wide", split_axis=0, concat_axis=1, tiled=True)
    m_dev = by_order.shape[0]
    lat_count = by_order.shape[1]
    chan_dev = by_order.shape[3]
    deg_count = legendre.shape[1]
    coeffs = jnp.einsum(
        "mlx,mxk->mlk",
        legendre,
        by_order.reshape(m_dev, lat_count, 2 * chan_dev),
        preferred_element_type=jnp.float32,
    )
    coeffs = coeffs.astype(jnp.bfloat16).reshape(m_dev, deg_count, 2, chan_dev)
    deg_dev = deg_count // lax.axis_size("narrow")
    gain_rows = lax.dynamic_slice_in_dim(
        filter_gain, lax.axis_index("narrow") * deg_dev, deg_dev, 0
    ).astype(jnp.float32)
    upper = jnp.concatenate([mix_real, mix_imag], axis=1)
    lower = jnp.concatenate([-mix_imag, mix_real], axis=1)
    wide_block = jnp.concatenate([upper, lower], axis=0)
    fragment = lax.all_to_all(coeffs, "narrow", split_axis=1, concat_axis=3, tiled=True)
    frag_count = fragment.shape[0]
    chan_all = fragment.shape[3]
    flat_rows = fragment.reshape(frag_count * deg_dev, 2 * chan_all)
    product = jnp.dot(flat_rows, wide_block, preferred_element_type=jnp.float32)
    product = product.reshape(frag_count, deg_dev, 2, chan_all) * gain_rows[None, :, None, :]
    mixed_coeffs = product.astype(jnp.bfloat16)
    back_coeffs = lax.all_to_all(mixed_coeffs, "narrow", split_axis=3, concat_axis=1, tiled=True)
    synthesis = jnp.einsum(
        "mlx,mlk->mxk",
        legendre,
        back_coeffs.reshape(m_dev, deg_count, 2 * chan_dev),
        preferred_element_type=jnp.float32,
    )
    synthesis = synthesis.astype(jnp.bfloat16).reshape(m_dev, lat_count, 2, chan_dev)
    by_latitude = lax.all_to_all(synthesis, "wide", split_axis=1, concat_axis=0, tiled=True)
    field_out = jnp.einsum(
        "kac,kn->acn", by_latitude[:, :, 0], cosine_table, preferred_element_type=jnp.float32
    )
    field_out = field_out - jnp.einsum(
        "kac,kn->acn", by_latitude[:, :, 1], sine_table, preferred_element_type=jnp.float32
    )
    return (field_out / math.sqrt(order_count)).astype(jnp.bfloat16)


def turn_cosine(phase, period):
    quarter = period // 4
    turns = jnp.floor(phase * (1.0 / quarter) + 0.5)
    angle = (phase - turns * quarter) * (2.0 * math.pi / period)
    quadrant = turns - 4.0 * jnp.floor(turns * 0.25)
    sq = angle * angle
    cosine = 1.0 + sq * (-0.5 + sq * (1.0 / 24 + sq * (-1.0 / 720 + sq * (1.0 / 40320))))
    sine = angle * (1.0 + sq * (-1.0 / 6 + sq * (1.0 / 120 + sq * (-1.0 / 5040 + sq * (1.0 / 362880)))))
    odd = (quadrant == 1.0) | (quadrant == 3.0)
    flip = (quadrant == 1.0) | (quadrant == 2.0)
    value = jnp.where(odd, sine, cosine)
    return jnp.where(flip, -value, value)


def spectral_kernel(
    dims, orders_hbm, quad_hbm, grid_hbm, leg_hbm, mixr_hbm, mixi_hbm, gain_hbm,
    out_ref, tabt_ref,
    grid_v, leg_v, mixr_v, mixi_v, gain_v, tab, spread, send1, recv1, lt, lf,
    weight, mixed, send2, recv2, flat2, orders_ref, quad_ref,
    grid_sem, in_sem, local_sem, s_send, s_recv, b_send, b_recv,
):
    n_wide, lat_dev, lon_count, chan, m_dev, deg_count = dims
    order_count = n_wide * m_dev
    rows = 2 * order_count
    rest = lat_dev - SUB
    half = n_wide * SUB
    pairs = lat_dev // 2
    others = m_dev * n_wide - 1
    me = lax.axis_index("wide")
    x = lax.axis_index("narrow")

    scalar_copies = []
    for i, (src, dst) in enumerate(((orders_hbm, orders_ref), (quad_hbm, quad_ref))):
        copy = pltpu.make_async_copy(src, dst, in_sem.at[4 + i])
        copy.start()
        scalar_copies.append(copy)
    grid_copies = []
    for p in range(pairs):
        copy = pltpu.make_async_copy(
            grid_hbm.at[pl.ds(2 * p, 2)], grid_v.at[pl.ds(2 * p, 2)], grid_sem.at[p]
        )
        copy.start()
        grid_copies.append(copy)
    in_copies = []
    for i, (src, dst) in enumerate(
        ((leg_hbm.at[x], leg_v), (mixr_hbm, mixr_v), (mixi_hbm, mixi_v), (gain_hbm, gain_v))
    ):
        copy = pltpu.make_async_copy(src, dst, in_sem.at[i])
        copy.start()
        in_copies.append(copy)

    steps = []
    bit = 1
    while bit < n_wide:
        steps.append(bit * (1 - 2 * (me // bit % 2)))
        bit *= 2

    def flipped(d):
        return me + functools.reduce(
            lambda a, b: a + b, [s for i, s in enumerate(steps) if d >> i & 1], 0
        )

    peers = []
    for d in reversed(range(n_wide)):
        for dx in (1, 0):
            if d or dx:
                peers.append((flipped(d), 1 - x if dx else x))

    barrier = pltpu.get_barrier_semaphore()
    for to in peers:
        pl.semaphore_signal(barrier, inc=1, device_id=to, device_id_type=MESH)

    for copy in scalar_copies:
        copy.wait()
    row = lax.broadcasted_iota(jnp.int32, (rows, LANES), 0)
    lane = lax.broadcasted_iota(jnp.int32, (rows, LANES), 1)
    block_rows = 2 * n_wide
    order_row = jnp.zeros((rows, LANES), jnp.int32)
    for j in range(m_dev):
        for w in range(n_wide):
            slot = orders_ref[w * m_dev + j]
            hit = (row == j * block_rows + w) | (row == j * block_rows + n_wide + w)
            order_row = jnp.where(hit, slot, order_row)
    shift = jnp.zeros((rows, LANES), jnp.int32)
    for j in range(m_dev):
        low = j * block_rows + n_wide
        shift = jnp.where((row >= low) & (row < low + n_wide), lon_count // 4, shift)
    for start in range(0, lon_count, LANES):
        size = min(LANES, lon_count - start)
        phase = (order_row * (lane + start) + shift).astype(jnp.float32)
        value = turn_cosine(phase, lon_count)
        tab[:, start:start + size] = value.astype(jnp.bfloat16)[:, :size]
        tabt_ref[start:start + size, :] = jnp.transpose(value)[:size].astype(jnp.bfloat16)

    factor = 1.0 / math.sqrt(lon_count)

    def transform(p):
        grid_copies[p].wait()
        rhs = jnp.concatenate([grid_v[2 * p], grid_v[2 * p + 1]], axis=1)
        res = jnp.dot(tab[...], rhs, preferred_element_type=jnp.float32)
        for i in range(2):
            a = 2 * p + i
            spread[a * rows:(a + 1) * rows, :] = res[:, i * chan:(i + 1) * chan] * (
                quad_ref[a] * factor
            )

    def row_of(j, ri, w):
        return j * block_rows + ri * n_wide + w

    heads, tails = pl.ds(0, 2), pl.ds(2, 1)

    def out_copy(part, to):
        where = tails if part else heads
        return pltpu.make_async_remote_copy(
            src_ref=send1.at[to[1] * n_wide + to[0], where],
            dst_ref=recv1.at[x * n_wide + me, where],
            send_sem=s_send.at[part],
            recv_sem=s_recv.at[part],
            device_id=to,
            device_id_type=MESH,
        )

    def own_copy(part):
        where = tails if part else heads
        mine = x * n_wide + me
        return pltpu.make_async_copy(
            send1.at[mine, where], recv1.at[mine, where], local_sem.at[part]
        )

    for p in range(SUB // 2):
        transform(p)
    for j in range(m_dev):
        for w in range(n_wide):
            for ri in range(2):
                send1[j * n_wide + w, ri] = spread[
                    pl.ds(row_of(j, ri, w), SUB, stride=rows), :
                ].astype(jnp.bfloat16)
    pl.semaphore_wait(barrier, others)
    for to in peers:
        out_copy(0, to).start()
    own_copy(0).start()

    for p in range(SUB // 2, pairs):
        transform(p)
    for j in range(m_dev):
        for w in range(n_wide):
            both = [
                spread[pl.ds(SUB * rows + row_of(j, ri, w), rest, stride=rows), :]
                for ri in range(2)
            ]
            send1[j * n_wide + w, 2] = jnp.concatenate(both, axis=0).astype(jnp.bfloat16)
    for to in peers:
        out_copy(1, to).start()
    own_copy(1).start()

    for copy in in_copies:
        copy.wait()
    lat_count = n_wide * lat_dev
    slot = lax.broadcasted_iota(jnp.int32, (2 * half, lat_count), 0)
    lat = lax.broadcasted_iota(jnp.int32, (2 * half, lat_count), 1)
    local = slot % SUB
    device = jnp.where(slot < half, slot, slot - half) // SUB
    want = device * lat_dev + jnp.where(slot < half, local, SUB + local % rest)
    pick = (want == lat).astype(jnp.bfloat16)
    moved = jnp.dot(pick, leg_v[...], preferred_element_type=jnp.float32)
    lt[...] = moved.astype(jnp.bfloat16)
    lf[...] = jnp.transpose(moved).astype(jnp.bfloat16)
    for i in range(m_dev):
        for o in range(m_dev):
            re = mixr_v[i * chan:(i + 1) * chan, o * chan:(o + 1) * chan]
            im = mixi_v[i * chan:(i + 1) * chan, o * chan:(o + 1) * chan]
            top, left = 2 * i * chan, 2 * o * chan
            weight[top:top + chan, left:left + chan] = re
            weight[top:top + chan, left + chan:left + 2 * chan] = im
            weight[top + chan:top + 2 * chan, left:left + chan] = -im
            weight[top + chan:top + 2 * chan, left + chan:left + 2 * chan] = re

    def all_arrived(buf, where, sem):
        piece = buf.at[pl.ds(0, others), where]
        pltpu.make_async_copy(piece, piece, sem).wait()

    for part, where in enumerate((heads, tails)):
        own_copy(part).wait()
        all_arrived(recv1, where, s_recv.at[part])

    tail_row = lax.broadcasted_iota(jnp.int32, (half, chan), 0) % SUB
    upper = tail_row < rest
    columns = []
    for i in range(m_dev):
        mine = pl.ds(i * n_wide, n_wide)
        tail = recv1[mine, 2].reshape(half, chan)
        for ri in range(2):
            head = recv1[mine, ri].reshape(half, chan)
            keep = upper if ri == 0 else jnp.logical_not(upper)
            columns.append(
                jnp.concatenate([head, jnp.where(keep, tail, jnp.zeros_like(tail))], axis=0)
            )
    spec = jnp.concatenate(columns, axis=1)
    coeffs = jnp.dot(lf[...], spec, preferred_element_type=jnp.float32).astype(jnp.bfloat16)

    def back_copy(to):
        return pltpu.make_async_remote_copy(
            src_ref=send2.at[to[1] * n_wide + to[0]],
            dst_ref=recv2.at[x * n_wide + me],
            send_sem=b_send,
            recv_sem=b_recv,
            device_id=to,
            device_id_type=MESH,
        )

    for o in range(m_dev):
        cols = pl.ds(2 * o * chan, 2 * chan)
        product = jnp.dot(coeffs, weight[:, cols], preferred_element_type=jnp.float32)
        gain = gain_v[:, o * chan:(o + 1) * chan].astype(jnp.float32)
        gain = jnp.concatenate([gain, gain], axis=1)
        mixed[o] = (product * gain).astype(jnp.bfloat16)
        syn = jnp.dot(lt[...], mixed[o], preferred_element_type=jnp.float32)
        re, im = syn[:, :chan], syn[:, chan:]
        mine = pl.ds(o * n_wide, n_wide)
        tail = jnp.where(upper, re[half:], im[half:])
        for t, tile in enumerate((re[:half], im[:half], tail)):
            send2[mine, t] = tile.astype(jnp.bfloat16).reshape(n_wide, SUB, chan)
        for w in range(n_wide):
            @pl.when((w != me) | (o != x))
            def _():
                back_copy((w, o)).start()

    mine = x * n_wide + me
    own_back = pltpu.make_async_copy(send2.at[mine], recv2.at[mine], local_sem.at[2])
    own_back.start()
    for part, where in enumerate((heads, tails)):
        all_arrived(send1, where, s_send.at[part])
    own_back.wait()
    everything = pl.ds(0, 3)
    all_arrived(recv2, everything, b_recv)
    flat2[...] = recv2[...].astype(jnp.float32).reshape(rows * 3 * SUB // 2, chan)
    for a in range(lat_dev):
        for j in range(m_dev):
            for ri in range(2):
                at = ri * SUB + a if a < SUB else 2 * SUB + ri * rest + a - SUB
                top = row_of(j, ri, 0)
                out_ref[a, top:top + n_wide, :] = flat2[
                    pl.ds(j * n_wide * 3 * SUB + at, n_wide, stride=3 * SUB), :
                ].astype(jnp.bfloat16)
    all_arrived(send2, everything, b_send)


def field_kernel(scale, tabt_ref, syn_ref, out_hbm, held, sem):
    lat_dev, _, chan = held.shape
    copies = []
    for p in range(lat_dev // 2):
        rhs = jnp.concatenate([syn_ref[2 * p], syn_ref[2 * p + 1]], axis=1)
        res = jnp.dot(tabt_ref[...], rhs, preferred_element_type=jnp.float32) * scale
        res = res.astype(jnp.bfloat16)
        held[2 * p] = res[:, :chan]
        held[2 * p + 1] = res[:, chan:]
        both = pl.ds(2 * p, 2)
        copy = pltpu.make_async_copy(held.at[both], out_hbm.at[both], sem.at[p])
        copy.start()
        copies.append(copy)
    for copy in copies:
        copy.wait()


def fast_shards(grid, quad_weights, orders, legendre, mix_real, mix_imag, filter_gain):
    lat_dev, chan, lon_count = grid.shape
    order_count = orders.shape[0]
    m_dev, deg_count, lat_count = legendre.shape
    n_wide = lax.axis_size("wide")
    rows = 2 * order_count
    half = n_wide * SUB
    bf16, f32 = jnp.bfloat16, jnp.float32
    vmem = pl.BlockSpec(memory_space=pltpu.VMEM)
    hbm = pl.BlockSpec(memory_space=pltpu.HBM)
    dims = (n_wide, lat_dev, lon_count, chan, m_dev, deg_count)
    chan_all = mix_real.shape[0]
    dma = pltpu.SemaphoreType.DMA
    synthesis, table = pl.pallas_call(
        functools.partial(spectral_kernel, dims),
        out_shape=(
            jax.ShapeDtypeStruct((lat_dev, rows, chan), bf16),
            jax.ShapeDtypeStruct((lon_count, rows), bf16),
        ),
        in_specs=[hbm] * 7,
        out_specs=(vmem, vmem),
        scratch_shapes=[
            pltpu.VMEM((lat_dev, lon_count, chan), bf16),
            pltpu.VMEM((lat_count, deg_count), bf16),
            pltpu.VMEM((chan_all, chan_all), bf16),
            pltpu.VMEM((chan_all, chan_all), bf16),
            pltpu.VMEM((deg_count, chan_all), bf16),
            pltpu.VMEM((rows, lon_count), bf16),
            pltpu.VMEM((lat_dev * rows, chan), f32),
            pltpu.VMEM((order_count, 3, SUB, chan), bf16),
            pltpu.VMEM((order_count, 3, SUB, chan), bf16),
            pltpu.VMEM((2 * half, deg_count), bf16),
            pltpu.VMEM((deg_count, 2 * half), bf16),
            pltpu.VMEM((4 * chan, 4 * chan), bf16),
            pltpu.VMEM((m_dev, deg_count, 2 * chan), bf16),
            pltpu.VMEM((order_count, 3, SUB, chan), bf16),
            pltpu.VMEM((order_count, 3, SUB, chan), bf16),
            pltpu.VMEM((order_count * 3 * SUB, chan), f32),
            pltpu.SMEM((order_count,), jnp.int32),
            pltpu.SMEM((lat_dev,), f32),
            dma((lat_dev // 2,)),
            dma((6,)),
            dma((3,)),
            dma((2,)),
            dma((2,)),
            dma,
            dma,
        ],
        compiler_params=pltpu.CompilerParams(
            collective_id=0, has_side_effects=True, vmem_limit_bytes=40 * 2**20
        ),
        name="spectral",
    )(*(pltpu.with_memory_space_constraint(v, pltpu.HBM) for v in (
        orders, quad_weights, jnp.transpose(grid, (0, 2, 1)), jnp.transpose(legendre, (0, 2, 1)),
        mix_real, mix_imag, filter_gain,
    )))
    field = pl.pallas_call(
        functools.partial(field_kernel, 1.0 / math.sqrt(order_count)),
        out_shape=jax.ShapeDtypeStruct((lat_dev, lon_count, chan), bf16),
        in_specs=[vmem, vmem],
        out_specs=pl.BlockSpec(memory_space=pl.ANY),
        scratch_shapes=[pltpu.VMEM((lat_dev, lon_count, chan), bf16), dma((lat_dev // 2,))],
        compiler_params=pltpu.CompilerParams(vmem_limit_bytes=24 * 2**20),
        name="field",
    )(table, synthesis)
    return jnp.transpose(field, (0, 2, 1))


def shards(grid, quad_weights, orders, legendre, mix_real, mix_imag, filter_gain):
    lat_dev, chan, lon_count = grid.shape
    m_dev = legendre.shape[0]
    n_wide = lax.axis_size("wide")
    rest = lat_dev - SUB
    fits = (
        lax.axis_size("narrow") == 2
        and chan == LANES
        and lon_count % 4 == 0
        and m_dev == 2
        and 2 * rest == SUB
        and lat_dev % 2 == 0
        and n_wide % 16 == 0
        and n_wide & (n_wide - 1) == 0
        and lon_count * lon_count < 2**24
    )
    body = fast_shards if fits else general_shards
    return body(grid, quad_weights, orders, legendre, mix_real, mix_imag, filter_gain)


def solution(mesh):
    placed = (P("wide", "narrow", None), P("wide"), P(), P("wide", None, None), P(), P(), P())
    return jax.shard_map(
        shards, mesh=mesh, in_specs=placed, out_specs=P("wide", "narrow", None), check_vma=False
    )
```

```python
import functools
import math

import jax
import jax.numpy as jnp
from jax import lax
from jax.experimental import pallas as pl
from jax.experimental.pallas import tpu as pltpu
from jax.sharding import PartitionSpec as P

MESH = pl.DeviceIdType.MESH
SUB = 8
LANES = 128


def fourier_tables(orders, lon_count):
    columns = jnp.arange(lon_count, dtype=jnp.int32)
    phase_int = orders[:, None] * columns[None, :] % lon_count
    angles = phase_int.astype(jnp.float32) * (2.0 * math.pi / lon_count)
    return (jnp.cos(angles).astype(jnp.bfloat16), jnp.sin(angles).astype(jnp.bfloat16))


def general_shards(grid, quad_weights, orders, legendre, mix_real, mix_imag, filter_gain):
    lon_count = grid.shape[2]
    order_count = orders.shape[0]
    cosine_table, sine_table = fourier_tables(orders, lon_count)
    factor = 1.0 / math.sqrt(lon_count)
    real_part = (
        jnp.einsum("acn,kn->kac", grid, cosine_table, preferred_element_type=jnp.float32) * factor
    )
    imag_part = (
        -jnp.einsum("acn,kn->kac", grid, sine_table, preferred_element_type=jnp.float32) * factor
    )
    spectra = (
        jnp.stack([real_part, imag_part], axis=2) * quad_weights[None, :, None, None]
    ).astype(jnp.bfloat16)
    by_order = lax.all_to_all(spectra, "wide", split_axis=0, concat_axis=1, tiled=True)
    m_dev = by_order.shape[0]
    lat_count = by_order.shape[1]
    chan_dev = by_order.shape[3]
    deg_count = legendre.shape[1]
    coeffs = jnp.einsum(
        "mlx,mxk->mlk",
        legendre,
        by_order.reshape(m_dev, lat_count, 2 * chan_dev),
        preferred_element_type=jnp.float32,
    )
    coeffs = coeffs.astype(jnp.bfloat16).reshape(m_dev, deg_count, 2, chan_dev)
    deg_dev = deg_count // lax.axis_size("narrow")
    gain_rows = lax.dynamic_slice_in_dim(
        filter_gain, lax.axis_index("narrow") * deg_dev, deg_dev, 0
    ).astype(jnp.float32)
    upper = jnp.concatenate([mix_real, mix_imag], axis=1)
    lower = jnp.concatenate([-mix_imag, mix_real], axis=1)
    wide_block = jnp.concatenate([upper, lower], axis=0)
    fragment = lax.all_to_all(coeffs, "narrow", split_axis=1, concat_axis=3, tiled=True)
    frag_count = fragment.shape[0]
    chan_all = fragment.shape[3]
    flat_rows = fragment.reshape(frag_count * deg_dev, 2 * chan_all)
    product = jnp.dot(flat_rows, wide_block, preferred_element_type=jnp.float32)
    product = product.reshape(frag_count, deg_dev, 2, chan_all) * gain_rows[None, :, None, :]
    mixed_coeffs = product.astype(jnp.bfloat16)
    back_coeffs = lax.all_to_all(mixed_coeffs, "narrow", split_axis=3, concat_axis=1, tiled=True)
    synthesis = jnp.einsum(
        "mlx,mlk->mxk",
        legendre,
        back_coeffs.reshape(m_dev, deg_count, 2 * chan_dev),
        preferred_element_type=jnp.float32,
    )
    synthesis = synthesis.astype(jnp.bfloat16).reshape(m_dev, lat_count, 2, chan_dev)
    by_latitude = lax.all_to_all(synthesis, "wide", split_axis=1, concat_axis=0, tiled=True)
    field_out = jnp.einsum(
        "kac,kn->acn", by_latitude[:, :, 0], cosine_table, preferred_element_type=jnp.float32
    )
    field_out = field_out - jnp.einsum(
        "kac,kn->acn", by_latitude[:, :, 1], sine_table, preferred_element_type=jnp.float32
    )
    return (field_out / math.sqrt(order_count)).astype(jnp.bfloat16)


def turn_both(phase, period):
    quarter = period // 4
    turns = jnp.floor(phase * (1.0 / quarter) + 0.5)
    angle = (phase - turns * quarter) * (2.0 * math.pi / period)
    quadrant = turns - 4.0 * jnp.floor(turns * 0.25)
    sq = angle * angle
    cosine = 1.0 + sq * (-0.5 + sq * (1.0 / 24 + sq * (-1.0 / 720 + sq * (1.0 / 40320))))
    sine = angle * (1.0 + sq * (-1.0 / 6 + sq * (1.0 / 120 + sq * (-1.0 / 5040 + sq * (1.0 / 362880)))))
    odd = (quadrant == 1.0) | (quadrant == 3.0)
    first = jnp.where(odd, sine, cosine)
    second = jnp.where(odd, cosine, sine)
    first = jnp.where((quadrant == 1.0) | (quadrant == 2.0), -first, first)
    second = jnp.where(quadrant >= 2.0, -second, second)
    return first, second


def rotate(pair, by):
    return pair[0] * by[0] - pair[1] * by[1], pair[1] * by[0] + pair[0] * by[1]


def spectral_kernel(
    dims, orders_hbm, quad_hbm, grid_hbm, leg_hbm, mixr_hbm, mixi_hbm, gain_hbm,
    out_ref, tabt_ref,
    grid_v, leg_v, mixr_v, mixi_v, gain_v, tab, spread, send1, recv1, lt, lf,
    weight, partial, mixed, send2, recv2, flat2, orders_ref, quad_ref,
    grid_sem, in_sem, local_sem, s_send, s_recv, b_send, b_recv,
):
    n_wide, lat_dev, lon_count, chan, m_dev, deg_count = dims
    order_count = n_wide * m_dev
    rows = 2 * order_count
    rest = lat_dev - SUB
    half = n_wide * SUB
    pairs = lat_dev // 2
    others = m_dev * n_wide - 1
    me = lax.axis_index("wide")
    x = lax.axis_index("narrow")

    steps = []
    bit = 1
    while bit < n_wide:
        steps.append(bit * (1 - 2 * (me // bit % 2)))
        bit *= 2

    def flipped(d):
        return me + functools.reduce(
            lambda a, b: a + b, [s for i, s in enumerate(steps) if d >> i & 1], 0
        )

    partner = 1 - x
    across = [(flipped(d), partner) for d in reversed(range(n_wide))]
    along = [(flipped(d), x) for d in reversed(range(1, n_wide))]

    barrier = pltpu.get_barrier_semaphore()
    for d in range(n_wide):
        for to in (across[d:d + 1] + along[d:d + 1]):
            pl.semaphore_signal(barrier, inc=1, device_id=to, device_id_type=MESH)

    scalar_copies = []
    for i, (src, dst) in enumerate(((orders_hbm, orders_ref), (quad_hbm, quad_ref))):
        copy = pltpu.make_async_copy(src, dst, in_sem.at[4 + i])
        copy.start()
        scalar_copies.append(copy)
    grid_copies = []
    for p in range(pairs):
        copy = pltpu.make_async_copy(
            grid_hbm.at[pl.ds(2 * p, 2)], grid_v.at[pl.ds(2 * p, 2)], grid_sem.at[p]
        )
        copy.start()
        grid_copies.append(copy)

    for copy in scalar_copies:
        copy.wait()
    block_rows = 2 * n_wide
    sub = lax.broadcasted_iota(jnp.int32, (SUB, LANES), 0)
    pieces = []
    for j in range(m_dev):
        for low in range(0, n_wide, SUB):
            piece = jnp.zeros((SUB, LANES), jnp.int32)
            for i in range(SUB):
                piece = jnp.where(sub == i, orders_ref[(low + i) * m_dev + j], piece)
            pieces.append(piece)
    order_row = jnp.concatenate(pieces, axis=0)
    lane = lax.broadcasted_iota(jnp.int32, (order_count, LANES), 1)
    group = 4
    block = turn_both((order_row * lane).astype(jnp.float32), lon_count)
    one = turn_both((order_row * LANES).astype(jnp.float32), lon_count)
    far = turn_both((order_row * (group * LANES)).astype(jnp.float32), lon_count)
    for i, start in enumerate(range(0, lon_count, LANES)):
        size = min(LANES, lon_count - start)
        if i % group == 0:
            block = block if i == 0 else rotate(block, far)
            now = block
        else:
            now = rotate(now, one)
        for j in range(m_dev):
            here = slice(j * n_wide, (j + 1) * n_wide)
            top = j * block_rows
            tab[top:top + n_wide, start:start + size] = now[0][here, :size].astype(jnp.bfloat16)
            tab[top + n_wide:top + block_rows, start:start + size] = (
                -now[1][here, :size]
            ).astype(jnp.bfloat16)

    factor = 1.0 / math.sqrt(lon_count)

    def transform(p):
        grid_copies[p].wait()
        rhs = jnp.concatenate([grid_v[2 * p], grid_v[2 * p + 1]], axis=1)
        res = jnp.dot(tab[...], rhs, preferred_element_type=jnp.float32)
        for i in range(2):
            a = 2 * p + i
            spread[a * rows:(a + 1) * rows, :] = res[:, i * chan:(i + 1) * chan] * (
                quad_ref[a] * factor
            )

    def row_of(j, ri, w):
        return j * block_rows + ri * n_wide + w

    def out_copy(part, to):
        return pltpu.make_async_remote_copy(
            src_ref=send1.at[to[1] * n_wide + to[0]],
            dst_ref=recv1.at[x * n_wide + me],
            send_sem=s_send.at[part],
            recv_sem=s_recv.at[part],
            device_id=to,
            device_id_type=MESH,
        )

    mine = x * n_wide + me
    own_copy = pltpu.make_async_copy(send1.at[mine], recv1.at[mine], local_sem.at[0])

    def rearranged(a, count, j, w):
        first = a * rows
        return jnp.concatenate(
            [
                spread[pl.ds(first + row_of(j, ri, w), count, stride=rows), :]
                for ri in range(2)
            ],
            axis=0,
        ).astype(jnp.bfloat16)

    for p in range(SUB // 2):
        transform(p)
    in_copies = []
    for i, (src, dst) in enumerate(
        ((leg_hbm.at[x], leg_v), (mixr_hbm, mixr_v), (mixi_hbm, mixi_v), (gain_hbm, gain_v))
    ):
        copy = pltpu.make_async_copy(src, dst, in_sem.at[i])
        copy.start()
        in_copies.append(copy)
    for j in range(m_dev):
        for w in range(n_wide):
            send1[j * n_wide + w, :2] = rearranged(0, SUB, j, w).reshape(2, SUB, chan)
    for p in range(SUB // 2, pairs):
        transform(p)
    for j in range(m_dev):
        for w in range(n_wide):
            send1[j * n_wide + w, 2] = rearranged(SUB, rest, j, w)
    own_copy.start()
    pl.semaphore_wait(barrier, others)
    for dx in range(2):
        for w in reversed(range(n_wide)):
            if dx == 0:
                @pl.when(w != me)
                def _():
                    out_copy(0, (w, x)).start()
            else:
                out_copy(1, (w, partner)).start()

    for start in range(0, lon_count, LANES):
        size = min(LANES, lon_count - start)
        tabt_ref[start:start + size, :] = jnp.transpose(
            tab[:, start:start + size].astype(jnp.float32)
        ).astype(jnp.bfloat16)
    for copy in in_copies:
        copy.wait()
    lat_count = n_wide * lat_dev
    slot = lax.broadcasted_iota(jnp.int32, (2 * half, lat_count), 0)
    lat = lax.broadcasted_iota(jnp.int32, (2 * half, lat_count), 1)
    local = slot % SUB
    device = jnp.where(slot < half, slot, slot - half) // SUB
    want = device * lat_dev + jnp.where(slot < half, local, SUB + local % rest)
    pick = (want == lat).astype(jnp.bfloat16)
    moved = jnp.dot(pick, leg_v[...], preferred_element_type=jnp.float32)
    lt[...] = moved.astype(jnp.bfloat16)
    lf[...] = jnp.transpose(moved).astype(jnp.bfloat16)
    for i, who in enumerate((x, partner)):
        in_rows = pl.ds(pl.multiple_of(who * chan, chan), chan)
        for o in range(m_dev):
            re = mixr_v[in_rows, o * chan:(o + 1) * chan]
            im = mixi_v[in_rows, o * chan:(o + 1) * chan]
            top, left = 2 * i * chan, 2 * o * chan
            weight[top:top + chan, left:left + chan] = re
            weight[top:top + chan, left + chan:left + 2 * chan] = im
            weight[top + chan:top + 2 * chan, left:left + chan] = -im
            weight[top + chan:top + 2 * chan, left + chan:left + 2 * chan] = re

    def all_arrived(buf, count, sem):
        piece = buf.at[pl.ds(0, count)]
        pltpu.make_async_copy(piece, piece, sem).wait()

    tail_row = lax.broadcasted_iota(jnp.int32, (half, chan), 0) % SUB
    upper = tail_row < rest

    def analysed(who):
        from_there = pl.ds(who * n_wide, n_wide)
        tail = recv1[from_there, 2].reshape(half, chan)
        columns = []
        for ri in range(2):
            head = recv1[from_there, ri].reshape(half, chan)
            keep = upper if ri == 0 else jnp.logical_not(upper)
            columns.append(
                jnp.concatenate([head, jnp.where(keep, tail, jnp.zeros_like(tail))], axis=0)
            )
        spec = jnp.concatenate(columns, axis=1)
        return jnp.dot(lf[...], spec, preferred_element_type=jnp.float32).astype(jnp.bfloat16)

    own_copy.wait()
    all_arrived(recv1, n_wide - 1, s_recv.at[0])
    coeffs = analysed(x)
    partial[...] = jnp.dot(coeffs, weight[:2 * chan], preferred_element_type=jnp.float32)
    all_arrived(recv1, n_wide, s_recv.at[1])
    coeffs = analysed(partner)

    def back_copy(to):
        return pltpu.make_async_remote_copy(
            src_ref=send2.at[to[1] * n_wide + to[0]],
            dst_ref=recv2.at[x * n_wide + me],
            send_sem=b_send,
            recv_sem=b_recv,
            device_id=to,
            device_id_type=MESH,
        )

    for o in range(m_dev):
        cols = pl.ds(2 * o * chan, 2 * chan)
        product = partial[:, cols] + jnp.dot(
            coeffs, weight[2 * chan:, cols], preferred_element_type=jnp.float32
        )
        gain = gain_v[:, o * chan:(o + 1) * chan].astype(jnp.float32)
        gain = jnp.concatenate([gain, gain], axis=1)
        mixed[o] = (product * gain).astype(jnp.bfloat16)
        syn = jnp.dot(lt[...], mixed[o], preferred_element_type=jnp.float32)
        re, im = syn[:, :chan], syn[:, chan:]
        mine = pl.ds(o * n_wide, n_wide)
        tail = jnp.where(upper, re[half:], im[half:])
        for t, tile in enumerate((re[:half], im[:half], tail)):
            send2[mine, t] = tile.astype(jnp.bfloat16).reshape(n_wide, SUB, chan)
        for w in range(n_wide):
            @pl.when((w != me) | (o != x))
            def _():
                back_copy((w, o)).start()

    mine = x * n_wide + me
    own_back = pltpu.make_async_copy(send2.at[mine], recv2.at[mine], local_sem.at[1])
    own_back.start()
    all_arrived(send1, n_wide - 1, s_send.at[0])
    all_arrived(send1, n_wide, s_send.at[1])
    own_back.wait()
    all_arrived(recv2, others, b_recv)
    flat2[...] = recv2[...].astype(jnp.float32).reshape(rows * 3 * SUB // 2, chan)
    for a in range(lat_dev):
        for j in range(m_dev):
            for ri in range(2):
                at = ri * SUB + a if a < SUB else 2 * SUB + ri * rest + a - SUB
                top = row_of(j, ri, 0)
                out_ref[a, top:top + n_wide, :] = flat2[
                    pl.ds(j * n_wide * 3 * SUB + at, n_wide, stride=3 * SUB), :
                ].astype(jnp.bfloat16)
    all_arrived(send2, others, b_send)


def field_kernel(scale, tabt_ref, syn_ref, out_hbm, held, sem):
    lat_dev, _, chan = held.shape
    copies = []
    for p in range(lat_dev // 2):
        rhs = jnp.concatenate([syn_ref[2 * p], syn_ref[2 * p + 1]], axis=1)
        res = jnp.dot(tabt_ref[...], rhs, preferred_element_type=jnp.float32) * scale
        res = res.astype(jnp.bfloat16)
        held[2 * p] = res[:, :chan]
        held[2 * p + 1] = res[:, chan:]
        both = pl.ds(2 * p, 2)
        copy = pltpu.make_async_copy(held.at[both], out_hbm.at[both], sem.at[p])
        copy.start()
        copies.append(copy)
    for copy in copies:
        copy.wait()


def fast_shards(grid, quad_weights, orders, legendre, mix_real, mix_imag, filter_gain):
    lat_dev, chan, lon_count = grid.shape
    order_count = orders.shape[0]
    m_dev, deg_count, lat_count = legendre.shape
    n_wide = lax.axis_size("wide")
    rows = 2 * order_count
    half = n_wide * SUB
    bf16, f32 = jnp.bfloat16, jnp.float32
    vmem = pl.BlockSpec(memory_space=pltpu.VMEM)
    hbm = pl.BlockSpec(memory_space=pltpu.HBM)
    dims = (n_wide, lat_dev, lon_count, chan, m_dev, deg_count)
    chan_all = mix_real.shape[0]
    dma = pltpu.SemaphoreType.DMA
    synthesis, table = pl.pallas_call(
        functools.partial(spectral_kernel, dims),
        out_shape=(
            jax.ShapeDtypeStruct((lat_dev, rows, chan), bf16),
            jax.ShapeDtypeStruct((lon_count, rows), bf16),
        ),
        in_specs=[hbm] * 7,
        out_specs=(vmem, vmem),
        scratch_shapes=[
            pltpu.VMEM((lat_dev, lon_count, chan), bf16),
            pltpu.VMEM((lat_count, deg_count), bf16),
            pltpu.VMEM((chan_all, chan_all), bf16),
            pltpu.VMEM((chan_all, chan_all), bf16),
            pltpu.VMEM((deg_count, chan_all), bf16),
            pltpu.VMEM((rows, lon_count), bf16),
            pltpu.VMEM((lat_dev * rows, chan), f32),
            pltpu.VMEM((order_count, 3, SUB, chan), bf16),
            pltpu.VMEM((order_count, 3, SUB, chan), bf16),
            pltpu.VMEM((2 * half, deg_count), bf16),
            pltpu.VMEM((deg_count, 2 * half), bf16),
            pltpu.VMEM((4 * chan, 4 * chan), bf16),
            pltpu.VMEM((deg_count, 4 * chan), f32),
            pltpu.VMEM((m_dev, deg_count, 2 * chan), bf16),
            pltpu.VMEM((order_count, 3, SUB, chan), bf16),
            pltpu.VMEM((order_count, 3, SUB, chan), bf16),
            pltpu.VMEM((order_count * 3 * SUB, chan), f32),
            pltpu.SMEM((order_count,), jnp.int32),
            pltpu.SMEM((lat_dev,), f32),
            dma((lat_dev // 2,)),
            dma((6,)),
            dma((2,)),
            dma((2,)),
            dma((2,)),
            dma,
            dma,
        ],
        compiler_params=pltpu.CompilerParams(
            collective_id=0, has_side_effects=True, vmem_limit_bytes=40 * 2**20
        ),
        name="spectral",
    )(*(pltpu.with_memory_space_constraint(v, pltpu.HBM) for v in (
        orders, quad_weights, jnp.transpose(grid, (0, 2, 1)), jnp.transpose(legendre, (0, 2, 1)),
        mix_real, mix_imag, filter_gain,
    )))
    field = pl.pallas_call(
        functools.partial(field_kernel, 1.0 / math.sqrt(order_count)),
        out_shape=jax.ShapeDtypeStruct((lat_dev, lon_count, chan), bf16),
        in_specs=[vmem, vmem],
        out_specs=pl.BlockSpec(memory_space=pl.ANY),
        scratch_shapes=[pltpu.VMEM((lat_dev, lon_count, chan), bf16), dma((lat_dev // 2,))],
        compiler_params=pltpu.CompilerParams(vmem_limit_bytes=24 * 2**20),
        name="field",
    )(table, synthesis)
    return jnp.transpose(field, (0, 2, 1))


def shards(grid, quad_weights, orders, legendre, mix_real, mix_imag, filter_gain):
    lat_dev, chan, lon_count = grid.shape
    m_dev = legendre.shape[0]
    n_wide = lax.axis_size("wide")
    rest = lat_dev - SUB
    fits = (
        lax.axis_size("narrow") == 2
        and chan == LANES
        and lon_count % 4 == 0
        and m_dev == 2
        and 2 * rest == SUB
        and lat_dev % 2 == 0
        and n_wide % 16 == 0
        and n_wide & (n_wide - 1) == 0
        and lon_count * lon_count < 2**24
    )
    body = fast_shards if fits else general_shards
    return body(grid, quad_weights, orders, legendre, mix_real, mix_imag, filter_gain)


def solution(mesh):
    placed = (P("wide", "narrow", None), P("wide"), P(), P("wide", None, None), P(), P(), P())
    return jax.shard_map(
        shards, mesh=mesh, in_specs=placed, out_specs=P("wide", "narrow", None), check_vma=False
    )
```

```python
import functools
import math

import jax
import jax.numpy as jnp
from jax import lax
from jax.experimental import pallas as pl
from jax.experimental.pallas import tpu as pltpu
from jax.sharding import PartitionSpec as P

MESH = pl.DeviceIdType.MESH
SUB = 8
LANES = 128


def fourier_tables(orders, lon_count):
    columns = jnp.arange(lon_count, dtype=jnp.int32)
    phase_int = orders[:, None] * columns[None, :] % lon_count
    angles = phase_int.astype(jnp.float32) * (2.0 * math.pi / lon_count)
    return (jnp.cos(angles).astype(jnp.bfloat16), jnp.sin(angles).astype(jnp.bfloat16))


def general_shards(grid, quad_weights, orders, legendre, mix_real, mix_imag, filter_gain):
    lon_count = grid.shape[2]
    order_count = orders.shape[0]
    cosine_table, sine_table = fourier_tables(orders, lon_count)
    factor = 1.0 / math.sqrt(lon_count)
    real_part = (
        jnp.einsum("acn,kn->kac", grid, cosine_table, preferred_element_type=jnp.float32) * factor
    )
    imag_part = (
        -jnp.einsum("acn,kn->kac", grid, sine_table, preferred_element_type=jnp.float32) * factor
    )
    spectra = (
        jnp.stack([real_part, imag_part], axis=2) * quad_weights[None, :, None, None]
    ).astype(jnp.bfloat16)
    by_order = lax.all_to_all(spectra, "wide", split_axis=0, concat_axis=1, tiled=True)
    m_dev = by_order.shape[0]
    lat_count = by_order.shape[1]
    chan_dev = by_order.shape[3]
    deg_count = legendre.shape[1]
    coeffs = jnp.einsum(
        "mlx,mxk->mlk",
        legendre,
        by_order.reshape(m_dev, lat_count, 2 * chan_dev),
        preferred_element_type=jnp.float32,
    )
    coeffs = coeffs.astype(jnp.bfloat16).reshape(m_dev, deg_count, 2, chan_dev)
    deg_dev = deg_count // lax.axis_size("narrow")
    gain_rows = lax.dynamic_slice_in_dim(
        filter_gain, lax.axis_index("narrow") * deg_dev, deg_dev, 0
    ).astype(jnp.float32)
    upper = jnp.concatenate([mix_real, mix_imag], axis=1)
    lower = jnp.concatenate([-mix_imag, mix_real], axis=1)
    wide_block = jnp.concatenate([upper, lower], axis=0)
    fragment = lax.all_to_all(coeffs, "narrow", split_axis=1, concat_axis=3, tiled=True)
    frag_count = fragment.shape[0]
    chan_all = fragment.shape[3]
    flat_rows = fragment.reshape(frag_count * deg_dev, 2 * chan_all)
    product = jnp.dot(flat_rows, wide_block, preferred_element_type=jnp.float32)
    product = product.reshape(frag_count, deg_dev, 2, chan_all) * gain_rows[None, :, None, :]
    mixed_coeffs = product.astype(jnp.bfloat16)
    back_coeffs = lax.all_to_all(mixed_coeffs, "narrow", split_axis=3, concat_axis=1, tiled=True)
    synthesis = jnp.einsum(
        "mlx,mlk->mxk",
        legendre,
        back_coeffs.reshape(m_dev, deg_count, 2 * chan_dev),
        preferred_element_type=jnp.float32,
    )
    synthesis = synthesis.astype(jnp.bfloat16).reshape(m_dev, lat_count, 2, chan_dev)
    by_latitude = lax.all_to_all(synthesis, "wide", split_axis=1, concat_axis=0, tiled=True)
    field_out = jnp.einsum(
        "kac,kn->acn", by_latitude[:, :, 0], cosine_table, preferred_element_type=jnp.float32
    )
    field_out = field_out - jnp.einsum(
        "kac,kn->acn", by_latitude[:, :, 1], sine_table, preferred_element_type=jnp.float32
    )
    return (field_out / math.sqrt(order_count)).astype(jnp.bfloat16)


def turn_both(phase, period):
    quarter = period // 4
    turns = jnp.floor(phase * (1.0 / quarter) + 0.5)
    angle = (phase - turns * quarter) * (2.0 * math.pi / period)
    quadrant = turns - 4.0 * jnp.floor(turns * 0.25)
    sq = angle * angle
    cosine = 1.0 + sq * (-0.5 + sq * (1.0 / 24 + sq * (-1.0 / 720 + sq * (1.0 / 40320))))
    sine = angle * (1.0 + sq * (-1.0 / 6 + sq * (1.0 / 120 + sq * (-1.0 / 5040 + sq * (1.0 / 362880)))))
    odd = (quadrant == 1.0) | (quadrant == 3.0)
    first = jnp.where(odd, sine, cosine)
    second = jnp.where(odd, cosine, sine)
    first = jnp.where((quadrant == 1.0) | (quadrant == 2.0), -first, first)
    second = jnp.where(quadrant >= 2.0, -second, second)
    return first, second


def rotate(pair, by):
    return pair[0] * by[0] - pair[1] * by[1], pair[1] * by[0] + pair[0] * by[1]


def spectral_kernel(
    dims, orders_hbm, quad_hbm, grid_hbm, leg_hbm, mixr_hbm, mixi_hbm, gain_hbm,
    out_ref, tabt_ref,
    grid_v, leg_v, mixr_v, mixi_v, gain_v, tab, spread, send1, recv1, lt, lf,
    weight, partial, mixed, send2, recv2, flat2, orders_ref, quad_ref,
    grid_sem, in_sem, local_sem, s_send, s_recv, b_send, b_recv, ready,
):
    n_wide, lat_dev, lon_count, chan, m_dev, deg_count = dims
    order_count = n_wide * m_dev
    rows = 2 * order_count
    rest = lat_dev - SUB
    half = n_wide * SUB
    pairs = lat_dev // 2
    others = m_dev * n_wide - 1
    me = lax.axis_index("wide")
    x = lax.axis_index("narrow")

    steps = []
    bit = 1
    while bit < n_wide:
        steps.append(bit * (1 - 2 * (me // bit % 2)))
        bit *= 2

    def flipped(d):
        return me + functools.reduce(
            lambda a, b: a + b, [s for i, s in enumerate(steps) if d >> i & 1], 0
        )

    partner = 1 - x
    across = [(flipped(d), partner) for d in reversed(range(n_wide))]
    along = [(flipped(d), x) for d in reversed(range(1, n_wide))]

    late_low = n_wide - n_wide // 4
    late = me >= late_low
    barrier = pltpu.get_barrier_semaphore()

    @pl.when(jnp.logical_not(late))
    def _():
        for d in range(n_wide):
            for to in across[d:d + 1] + along[d:d + 1]:
                pl.semaphore_signal(barrier, inc=1, device_id=to, device_id_type=MESH)

    @pl.when(late)
    def _():
        for d in reversed(range(n_wide // 4)):
            for to in (flipped(d), partner), (flipped(d), x):
                if d or to[1] is partner:
                    pl.semaphore_signal(barrier, inc=1, device_id=to, device_id_type=MESH)

    scalar_copies = []
    for i, (src, dst) in enumerate(((orders_hbm, orders_ref), (quad_hbm, quad_ref))):
        copy = pltpu.make_async_copy(src, dst, in_sem.at[4 + i])
        copy.start()
        scalar_copies.append(copy)
    grid_copies = []
    for p in range(pairs):
        copy = pltpu.make_async_copy(
            grid_hbm.at[pl.ds(2 * p, 2)], grid_v.at[pl.ds(2 * p, 2)], grid_sem.at[p]
        )
        copy.start()
        grid_copies.append(copy)

    for copy in scalar_copies:
        copy.wait()
    block_rows = 2 * n_wide
    sub = lax.broadcasted_iota(jnp.int32, (SUB, LANES), 0)
    pieces = []
    for j in range(m_dev):
        for low in range(0, n_wide, SUB):
            piece = jnp.zeros((SUB, LANES), jnp.int32)
            for i in range(SUB):
                piece = jnp.where(sub == i, orders_ref[(low + i) * m_dev + j], piece)
            pieces.append(piece)
    order_row = jnp.concatenate(pieces, axis=0)
    lane = lax.broadcasted_iota(jnp.int32, (order_count, LANES), 1)
    group = 4
    block = turn_both((order_row * lane).astype(jnp.float32), lon_count)
    one = turn_both((order_row * LANES).astype(jnp.float32), lon_count)
    far = turn_both((order_row * (group * LANES)).astype(jnp.float32), lon_count)
    for i, start in enumerate(range(0, lon_count, LANES)):
        size = min(LANES, lon_count - start)
        if i % group == 0:
            block = block if i == 0 else rotate(block, far)
            now = block
        else:
            now = rotate(now, one)
        for j in range(m_dev):
            here = slice(j * n_wide, (j + 1) * n_wide)
            top = j * block_rows
            tab[top:top + n_wide, start:start + size] = now[0][here, :size].astype(jnp.bfloat16)
            tab[top + n_wide:top + block_rows, start:start + size] = (
                -now[1][here, :size]
            ).astype(jnp.bfloat16)

    @pl.when(late)
    def _():
        pl.semaphore_wait(barrier, others)
        for w in range(3):
            pl.semaphore_signal(
                ready, inc=1, device_id=(w * (n_wide // 4) + me % (n_wide // 4), x),
                device_id_type=MESH,
            )

    factor = 1.0 / math.sqrt(lon_count)

    def transform(p):
        grid_copies[p].wait()
        rhs = jnp.concatenate([grid_v[2 * p], grid_v[2 * p + 1]], axis=1)
        res = jnp.dot(tab[...], rhs, preferred_element_type=jnp.float32)
        for i in range(2):
            a = 2 * p + i
            spread[a * rows:(a + 1) * rows, :] = res[:, i * chan:(i + 1) * chan] * (
                quad_ref[a] * factor
            )

    def row_of(j, ri, w):
        return j * block_rows + ri * n_wide + w

    def out_copy(part, to):
        return pltpu.make_async_remote_copy(
            src_ref=send1.at[to[1] * n_wide + to[0]],
            dst_ref=recv1.at[x * n_wide + me],
            send_sem=s_send.at[part],
            recv_sem=s_recv.at[part],
            device_id=to,
            device_id_type=MESH,
        )

    mine = x * n_wide + me
    own_copy = pltpu.make_async_copy(send1.at[mine], recv1.at[mine], local_sem.at[0])

    def rearranged(a, count, j, w):
        first = a * rows
        return jnp.concatenate(
            [
                spread[pl.ds(first + row_of(j, ri, w), count, stride=rows), :]
                for ri in range(2)
            ],
            axis=0,
        ).astype(jnp.bfloat16)

    for p in range(SUB // 2):
        transform(p)
    for j in range(m_dev):
        for w in range(n_wide):
            send1[j * n_wide + w, :2] = rearranged(0, SUB, j, w).reshape(2, SUB, chan)
    for p in range(SUB // 2, pairs):
        transform(p)
    for j in range(m_dev):
        for w in range(n_wide):
            send1[j * n_wide + w, 2] = rearranged(SUB, rest, j, w)
    in_copies = []
    for i, (src, dst) in enumerate(
        ((leg_hbm.at[x], leg_v), (mixr_hbm, mixr_v), (mixi_hbm, mixi_v), (gain_hbm, gain_v))
    ):
        copy = pltpu.make_async_copy(src, dst, in_sem.at[i])
        copy.start()
        in_copies.append(copy)
    own_copy.start()

    near = [i + (i >= me).astype(jnp.int32) for i in range(n_wide - 1)]
    chunk = n_wide // 4

    def send_to(low, count, near):
        for w in reversed(near):
            out_copy(0, (w, x)).start()
        for w in reversed(range(low, low + count)):
            out_copy(1, (w, partner)).start()

    def send_quarters(order, last):
        for q in order:
            low = q * chunk
            send_to(low, chunk, near[low:min(low + chunk, last)])

    @pl.when(late)
    def _():
        send_quarters((3, 2, 1, 0), n_wide - 1)

    @pl.when(jnp.logical_not(late))
    def _():
        pl.semaphore_wait(barrier, 2 * late_low - 1)

        @pl.when(me < n_wide // 2)
        def _():
            send_quarters((2, 1, 0), late_low - 1)

        @pl.when(me >= n_wide // 2)
        def _():
            send_quarters((2, 1, 0), late_low - 1)

        pl.semaphore_wait(ready, 1)
        send_to(late_low, n_wide - late_low, range(late_low, n_wide))

    for start in range(0, lon_count, LANES):
        size = min(LANES, lon_count - start)
        tabt_ref[start:start + size, :] = jnp.transpose(
            tab[:, start:start + size].astype(jnp.float32)
        ).astype(jnp.bfloat16)
    for copy in in_copies:
        copy.wait()
    lat_count = n_wide * lat_dev
    slot = lax.broadcasted_iota(jnp.int32, (2 * half, lat_count), 0)
    lat = lax.broadcasted_iota(jnp.int32, (2 * half, lat_count), 1)
    local = slot % SUB
    device = jnp.where(slot < half, slot, slot - half) // SUB
    want = device * lat_dev + jnp.where(slot < half, local, SUB + local % rest)
    pick = (want == lat).astype(jnp.bfloat16)
    moved = jnp.dot(pick, leg_v[...], preferred_element_type=jnp.float32)
    lt[...] = moved.astype(jnp.bfloat16)
    lf[...] = jnp.transpose(moved).astype(jnp.bfloat16)
    for i, who in enumerate((x, partner)):
        in_rows = pl.ds(pl.multiple_of(who * chan, chan), chan)
        for o in range(m_dev):
            re = mixr_v[in_rows, o * chan:(o + 1) * chan]
            im = mixi_v[in_rows, o * chan:(o + 1) * chan]
            top, left = 2 * i * chan, 2 * o * chan
            weight[top:top + chan, left:left + chan] = re
            weight[top:top + chan, left + chan:left + 2 * chan] = im
            weight[top + chan:top + 2 * chan, left:left + chan] = -im
            weight[top + chan:top + 2 * chan, left + chan:left + 2 * chan] = re

    def all_arrived(buf, count, sem):
        piece = buf.at[pl.ds(0, count)]
        pltpu.make_async_copy(piece, piece, sem).wait()

    tail_row = lax.broadcasted_iota(jnp.int32, (half, chan), 0) % SUB
    upper = tail_row < rest

    def analysed(who):
        from_there = pl.ds(who * n_wide, n_wide)
        tail = recv1[from_there, 2].reshape(half, chan)
        columns = []
        for ri in range(2):
            head = recv1[from_there, ri].reshape(half, chan)
            keep = upper if ri == 0 else jnp.logical_not(upper)
            columns.append(
                jnp.concatenate([head, jnp.where(keep, tail, jnp.zeros_like(tail))], axis=0)
            )
        spec = jnp.concatenate(columns, axis=1)
        return jnp.dot(lf[...], spec, preferred_element_type=jnp.float32).astype(jnp.bfloat16)

    own_copy.wait()
    all_arrived(recv1, n_wide - 1, s_recv.at[0])
    coeffs = analysed(x)
    partial[...] = jnp.dot(coeffs, weight[:2 * chan], preferred_element_type=jnp.float32)
    all_arrived(recv1, n_wide, s_recv.at[1])
    coeffs = analysed(partner)

    def back_copy(to):
        return pltpu.make_async_remote_copy(
            src_ref=send2.at[to[1] * n_wide + to[0]],
            dst_ref=recv2.at[x * n_wide + me],
            send_sem=b_send,
            recv_sem=b_recv,
            device_id=to,
            device_id_type=MESH,
        )

    for o in range(m_dev):
        cols = pl.ds(2 * o * chan, 2 * chan)
        product = partial[:, cols] + jnp.dot(
            coeffs, weight[2 * chan:, cols], preferred_element_type=jnp.float32
        )
        gain = gain_v[:, o * chan:(o + 1) * chan].astype(jnp.float32)
        gain = jnp.concatenate([gain, gain], axis=1)
        mixed[o] = (product * gain).astype(jnp.bfloat16)
        syn = jnp.dot(lt[...], mixed[o], preferred_element_type=jnp.float32)
        re, im = syn[:, :chan], syn[:, chan:]
        mine = pl.ds(o * n_wide, n_wide)
        tail = jnp.where(upper, re[half:], im[half:])
        for t, tile in enumerate((re[:half], im[:half], tail)):
            send2[mine, t] = tile.astype(jnp.bfloat16).reshape(n_wide, SUB, chan)
        for i in range(n_wide - 1):
            over = ((x == o) & (i >= me)).astype(jnp.int32)
            back_copy((i + over, o)).start()

        @pl.when(x != o)
        def _():
            back_copy((n_wide - 1, o)).start()

    mine = x * n_wide + me
    own_back = pltpu.make_async_copy(send2.at[mine], recv2.at[mine], local_sem.at[1])
    own_back.start()
    all_arrived(send1, n_wide - 1, s_send.at[0])
    all_arrived(send1, n_wide, s_send.at[1])
    own_back.wait()
    all_arrived(recv2, others, b_recv)
    flat2[...] = recv2[...].astype(jnp.float32).reshape(rows * 3 * SUB // 2, chan)
    for a in range(lat_dev):
        for j in range(m_dev):
            for ri in range(2):
                at = ri * SUB + a if a < SUB else 2 * SUB + ri * rest + a - SUB
                top = row_of(j, ri, 0)
                out_ref[a, top:top + n_wide, :] = flat2[
                    pl.ds(j * n_wide * 3 * SUB + at, n_wide, stride=3 * SUB), :
                ].astype(jnp.bfloat16)
    all_arrived(send2, others, b_send)


def field_kernel(scale, tabt_ref, syn_ref, out_hbm, held, sem):
    lat_dev, _, chan = held.shape
    copies = []
    for p in range(lat_dev // 2):
        rhs = jnp.concatenate([syn_ref[2 * p], syn_ref[2 * p + 1]], axis=1)
        res = jnp.dot(tabt_ref[...], rhs, preferred_element_type=jnp.float32) * scale
        res = res.astype(jnp.bfloat16)
        held[2 * p] = res[:, :chan]
        held[2 * p + 1] = res[:, chan:]
        both = pl.ds(2 * p, 2)
        copy = pltpu.make_async_copy(held.at[both], out_hbm.at[both], sem.at[p])
        copy.start()
        copies.append(copy)
    for copy in copies:
        copy.wait()


def fast_shards(grid, quad_weights, orders, legendre, mix_real, mix_imag, filter_gain):
    lat_dev, chan, lon_count = grid.shape
    order_count = orders.shape[0]
    m_dev, deg_count, lat_count = legendre.shape
    n_wide = lax.axis_size("wide")
    rows = 2 * order_count
    half = n_wide * SUB
    bf16, f32 = jnp.bfloat16, jnp.float32
    vmem = pl.BlockSpec(memory_space=pltpu.VMEM)
    hbm = pl.BlockSpec(memory_space=pltpu.HBM)
    dims = (n_wide, lat_dev, lon_count, chan, m_dev, deg_count)
    chan_all = mix_real.shape[0]
    dma = pltpu.SemaphoreType.DMA
    synthesis, table = pl.pallas_call(
        functools.partial(spectral_kernel, dims),
        out_shape=(
            jax.ShapeDtypeStruct((lat_dev, rows, chan), bf16),
            jax.ShapeDtypeStruct((lon_count, rows), bf16),
        ),
        in_specs=[hbm] * 7,
        out_specs=(vmem, vmem),
        scratch_shapes=[
            pltpu.VMEM((lat_dev, lon_count, chan), bf16),
            pltpu.VMEM((lat_count, deg_count), bf16),
            pltpu.VMEM((chan_all, chan_all), bf16),
            pltpu.VMEM((chan_all, chan_all), bf16),
            pltpu.VMEM((deg_count, chan_all), bf16),
            pltpu.VMEM((rows, lon_count), bf16),
            pltpu.VMEM((lat_dev * rows, chan), f32),
            pltpu.VMEM((order_count, 3, SUB, chan), bf16),
            pltpu.VMEM((order_count, 3, SUB, chan), bf16),
            pltpu.VMEM((2 * half, deg_count), bf16),
            pltpu.VMEM((deg_count, 2 * half), bf16),
            pltpu.VMEM((4 * chan, 4 * chan), bf16),
            pltpu.VMEM((deg_count, 4 * chan), f32),
            pltpu.VMEM((m_dev, deg_count, 2 * chan), bf16),
            pltpu.VMEM((order_count, 3, SUB, chan), bf16),
            pltpu.VMEM((order_count, 3, SUB, chan), bf16),
            pltpu.VMEM((order_count * 3 * SUB, chan), f32),
            pltpu.SMEM((order_count,), jnp.int32),
            pltpu.SMEM((lat_dev,), f32),
            dma((lat_dev // 2,)),
            dma((6,)),
            dma((2,)),
            dma((2,)),
            dma((2,)),
            dma,
            dma,
            pltpu.SemaphoreType.REGULAR,
        ],
        compiler_params=pltpu.CompilerParams(
            collective_id=0, has_side_effects=True, vmem_limit_bytes=40 * 2**20
        ),
        name="spectral",
    )(*(pltpu.with_memory_space_constraint(v, pltpu.HBM) for v in (
        orders, quad_weights, jnp.transpose(grid, (0, 2, 1)), jnp.transpose(legendre, (0, 2, 1)),
        mix_real, mix_imag, filter_gain,
    )))
    field = pl.pallas_call(
        functools.partial(field_kernel, 1.0 / math.sqrt(order_count)),
        out_shape=jax.ShapeDtypeStruct((lat_dev, lon_count, chan), bf16),
        in_specs=[vmem, vmem],
        out_specs=pl.BlockSpec(memory_space=pl.ANY),
        scratch_shapes=[pltpu.VMEM((lat_dev, lon_count, chan), bf16), dma((lat_dev // 2,))],
        compiler_params=pltpu.CompilerParams(vmem_limit_bytes=24 * 2**20),
        name="field",
    )(table, synthesis)
    return jnp.transpose(field, (0, 2, 1))


def shards(grid, quad_weights, orders, legendre, mix_real, mix_imag, filter_gain):
    lat_dev, chan, lon_count = grid.shape
    m_dev = legendre.shape[0]
    n_wide = lax.axis_size("wide")
    rest = lat_dev - SUB
    fits = (
        lax.axis_size("narrow") == 2
        and chan == LANES
        and lon_count % 4 == 0
        and m_dev == 2
        and 2 * rest == SUB
        and lat_dev % 2 == 0
        and n_wide % 16 == 0
        and n_wide & (n_wide - 1) == 0
        and lon_count * lon_count < 2**24
    )
    body = fast_shards if fits else general_shards
    return body(grid, quad_weights, orders, legendre, mix_real, mix_imag, filter_gain)


def solution(mesh):
    placed = (P("wide", "narrow", None), P("wide"), P(), P("wide", None, None), P(), P(), P())
    return jax.shard_map(
        shards, mesh=mesh, in_specs=placed, out_specs=P("wide", "narrow", None), check_vma=False
    )
```

```python
import functools
import math

import jax
import jax.numpy as jnp
from jax import lax
from jax.experimental import pallas as pl
from jax.experimental.pallas import tpu as pltpu
from jax.sharding import PartitionSpec as P

MESH = pl.DeviceIdType.MESH
SUB = 8
LANES = 128


def fourier_tables(orders, lon_count):
    columns = jnp.arange(lon_count, dtype=jnp.int32)
    phase_int = orders[:, None] * columns[None, :] % lon_count
    angles = phase_int.astype(jnp.float32) * (2.0 * math.pi / lon_count)
    return (jnp.cos(angles).astype(jnp.bfloat16), jnp.sin(angles).astype(jnp.bfloat16))


def general_shards(grid, quad_weights, orders, legendre, mix_real, mix_imag, filter_gain):
    lon_count = grid.shape[2]
    order_count = orders.shape[0]
    cosine_table, sine_table = fourier_tables(orders, lon_count)
    factor = 1.0 / math.sqrt(lon_count)
    real_part = (
        jnp.einsum("acn,kn->kac", grid, cosine_table, preferred_element_type=jnp.float32) * factor
    )
    imag_part = (
        -jnp.einsum("acn,kn->kac", grid, sine_table, preferred_element_type=jnp.float32) * factor
    )
    spectra = (
        jnp.stack([real_part, imag_part], axis=2) * quad_weights[None, :, None, None]
    ).astype(jnp.bfloat16)
    by_order = lax.all_to_all(spectra, "wide", split_axis=0, concat_axis=1, tiled=True)
    m_dev = by_order.shape[0]
    lat_count = by_order.shape[1]
    chan_dev = by_order.shape[3]
    deg_count = legendre.shape[1]
    coeffs = jnp.einsum(
        "mlx,mxk->mlk",
        legendre,
        by_order.reshape(m_dev, lat_count, 2 * chan_dev),
        preferred_element_type=jnp.float32,
    )
    coeffs = coeffs.astype(jnp.bfloat16).reshape(m_dev, deg_count, 2, chan_dev)
    deg_dev = deg_count // lax.axis_size("narrow")
    gain_rows = lax.dynamic_slice_in_dim(
        filter_gain, lax.axis_index("narrow") * deg_dev, deg_dev, 0
    ).astype(jnp.float32)
    upper = jnp.concatenate([mix_real, mix_imag], axis=1)
    lower = jnp.concatenate([-mix_imag, mix_real], axis=1)
    wide_block = jnp.concatenate([upper, lower], axis=0)
    fragment = lax.all_to_all(coeffs, "narrow", split_axis=1, concat_axis=3, tiled=True)
    frag_count = fragment.shape[0]
    chan_all = fragment.shape[3]
    flat_rows = fragment.reshape(frag_count * deg_dev, 2 * chan_all)
    product = jnp.dot(flat_rows, wide_block, preferred_element_type=jnp.float32)
    product = product.reshape(frag_count, deg_dev, 2, chan_all) * gain_rows[None, :, None, :]
    mixed_coeffs = product.astype(jnp.bfloat16)
    back_coeffs = lax.all_to_all(mixed_coeffs, "narrow", split_axis=3, concat_axis=1, tiled=True)
    synthesis = jnp.einsum(
        "mlx,mlk->mxk",
        legendre,
        back_coeffs.reshape(m_dev, deg_count, 2 * chan_dev),
        preferred_element_type=jnp.float32,
    )
    synthesis = synthesis.astype(jnp.bfloat16).reshape(m_dev, lat_count, 2, chan_dev)
    by_latitude = lax.all_to_all(synthesis, "wide", split_axis=1, concat_axis=0, tiled=True)
    field_out = jnp.einsum(
        "kac,kn->acn", by_latitude[:, :, 0], cosine_table, preferred_element_type=jnp.float32
    )
    field_out = field_out - jnp.einsum(
        "kac,kn->acn", by_latitude[:, :, 1], sine_table, preferred_element_type=jnp.float32
    )
    return (field_out / math.sqrt(order_count)).astype(jnp.bfloat16)


def turn_both(phase, period):
    quarter = period // 4
    turns = jnp.floor(phase * (1.0 / quarter) + 0.5)
    angle = (phase - turns * quarter) * (2.0 * math.pi / period)
    quadrant = turns - 4.0 * jnp.floor(turns * 0.25)
    sq = angle * angle
    cosine = 1.0 + sq * (-0.5 + sq * (1.0 / 24 + sq * (-1.0 / 720 + sq * (1.0 / 40320))))
    sine = angle * (1.0 + sq * (-1.0 / 6 + sq * (1.0 / 120 + sq * (-1.0 / 5040 + sq * (1.0 / 362880)))))
    odd = (quadrant == 1.0) | (quadrant == 3.0)
    first = jnp.where(odd, sine, cosine)
    second = jnp.where(odd, cosine, sine)
    first = jnp.where((quadrant == 1.0) | (quadrant == 2.0), -first, first)
    second = jnp.where(quadrant >= 2.0, -second, second)
    return first, second


def rotate(pair, by):
    return pair[0] * by[0] - pair[1] * by[1], pair[1] * by[0] + pair[0] * by[1]


def spectral_kernel(
    dims, orders_hbm, quad_hbm, grid_hbm, leg_hbm, mixr_hbm, mixi_hbm, gain_hbm,
    out_ref, tabt_ref,
    grid_v, leg_v, mixr_v, mixi_v, gain_v, tab, spread, send1, recv1, lt, lf,
    weight, partial, mixed, send2, recv2, flat2, orders_ref, quad_ref,
    grid_sem, in_sem, local_sem, s_send, s_recv, b_send, b_recv, ready,
):
    n_wide, lat_dev, lon_count, chan, m_dev, deg_count = dims
    order_count = n_wide * m_dev
    rows = 2 * order_count
    rest = lat_dev - SUB
    half = n_wide * SUB
    pairs = lat_dev // 2
    others = m_dev * n_wide - 1
    me = lax.axis_index("wide")
    x = lax.axis_index("narrow")

    steps = []
    bit = 1
    while bit < n_wide:
        steps.append(bit * (1 - 2 * (me // bit % 2)))
        bit *= 2

    def flipped(d):
        return me + functools.reduce(
            lambda a, b: a + b, [s for i, s in enumerate(steps) if d >> i & 1], 0
        )

    partner = 1 - x
    across = [(flipped(d), partner) for d in reversed(range(n_wide))]
    along = [(flipped(d), x) for d in reversed(range(1, n_wide))]

    scalar_copies = []
    for i, (src, dst) in enumerate(((orders_hbm, orders_ref), (quad_hbm, quad_ref))):
        copy = pltpu.make_async_copy(src, dst, in_sem.at[4 + i])
        copy.start()
        scalar_copies.append(copy)
    grid_copies = []
    for p in range(pairs):
        copy = pltpu.make_async_copy(
            grid_hbm.at[pl.ds(2 * p, 2)], grid_v.at[pl.ds(2 * p, 2)], grid_sem.at[p]
        )
        copy.start()
        grid_copies.append(copy)

    late_low = n_wide - n_wide // 4
    late = me >= late_low
    barrier = pltpu.get_barrier_semaphore()

    @pl.when(jnp.logical_not(late))
    def _():
        for d in range(n_wide):
            for to in across[d:d + 1] + along[d:d + 1]:
                pl.semaphore_signal(barrier, inc=1, device_id=to, device_id_type=MESH)

    @pl.when(late)
    def _():
        for d in reversed(range(n_wide // 4)):
            for to in (flipped(d), partner), (flipped(d), x):
                if d or to[1] is partner:
                    pl.semaphore_signal(barrier, inc=1, device_id=to, device_id_type=MESH)

    for copy in scalar_copies:
        copy.wait()
    block_rows = 2 * n_wide
    sub = lax.broadcasted_iota(jnp.int32, (SUB, LANES), 0)
    pieces = []
    for j in range(m_dev):
        for low in range(0, n_wide, SUB):
            piece = jnp.zeros((SUB, LANES), jnp.int32)
            for i in range(SUB):
                piece = jnp.where(sub == i, orders_ref[(low + i) * m_dev + j], piece)
            pieces.append(piece)
    order_row = jnp.concatenate(pieces, axis=0)
    lane = lax.broadcasted_iota(jnp.int32, (order_count, LANES), 1)
    group = 4
    block = turn_both((order_row * lane).astype(jnp.float32), lon_count)
    one = turn_both((order_row * LANES).astype(jnp.float32), lon_count)
    far = turn_both((order_row * (group * LANES)).astype(jnp.float32), lon_count)
    for i, start in enumerate(range(0, lon_count, LANES)):
        size = min(LANES, lon_count - start)
        if i % group == 0:
            block = block if i == 0 else rotate(block, far)
            now = block
        else:
            now = rotate(now, one)
        for j in range(m_dev):
            here = slice(j * n_wide, (j + 1) * n_wide)
            top = j * block_rows
            tab[top:top + n_wide, start:start + size] = now[0][here, :size].astype(jnp.bfloat16)
            tab[top + n_wide:top + block_rows, start:start + size] = (
                -now[1][here, :size]
            ).astype(jnp.bfloat16)

    @pl.when(late)
    def _():
        pl.semaphore_wait(barrier, others)
        for w in range(3):
            pl.semaphore_signal(
                ready, inc=1, device_id=(w * (n_wide // 4) + me % (n_wide // 4), x),
                device_id_type=MESH,
            )

    factor = 1.0 / math.sqrt(lon_count)

    def transform(p):
        grid_copies[p].wait()
        rhs = jnp.concatenate([grid_v[2 * p], grid_v[2 * p + 1]], axis=1)
        res = jnp.dot(tab[...], rhs, preferred_element_type=jnp.float32)
        for i in range(2):
            a = 2 * p + i
            spread[a * rows:(a + 1) * rows, :] = res[:, i * chan:(i + 1) * chan] * (
                quad_ref[a] * factor
            )

    def row_of(j, ri, w):
        return j * block_rows + ri * n_wide + w

    whole, heads, tails = pl.ds(0, 3), pl.ds(0, 2), pl.ds(2, 1)

    def out_copy(part, to, where):
        return pltpu.make_async_remote_copy(
            src_ref=send1.at[to[1] * n_wide + to[0], where],
            dst_ref=recv1.at[x * n_wide + me, where],
            send_sem=s_send.at[part],
            recv_sem=s_recv.at[part],
            device_id=to,
            device_id_type=MESH,
        )

    mine = x * n_wide + me
    own_copy = pltpu.make_async_copy(send1.at[mine], recv1.at[mine], local_sem.at[0])

    def rearranged(a, count, j, w):
        first = a * rows
        return jnp.concatenate(
            [
                spread[pl.ds(first + row_of(j, ri, w), count, stride=rows), :]
                for ri in range(2)
            ],
            axis=0,
        ).astype(jnp.bfloat16)

    chunk = n_wide // 4

    first = 2

    def send_first(where):
        for w in range(first):
            @pl.when((w != me) | (x > 0))
            def _():
                out_copy(x, (w, 0), where).start()

    def send_quarter(q, where):
        for part, side in enumerate((x, partner)):
            for w in reversed(range(q * chunk, (q + 1) * chunk)):
                wanted = (w != me) | (part > 0)
                if w < first:
                    wanted = wanted & (side > 0)

                @pl.when(wanted)
                def _():
                    out_copy(part, (w, side), where).start()

    def send_quarters(order, where):
        send_first(where)
        for q in order:
            send_quarter(q, where)

    for p in range(SUB // 2):
        transform(p)
    for j in range(m_dev):
        for w in range(n_wide):
            send1[j * n_wide + w, :2] = rearranged(0, SUB, j, w).reshape(2, SUB, chan)
    upper_half = me >= n_wide // 2

    @pl.when(upper_half)
    def _():
        @pl.when(late)
        def _():
            send_quarters((3, 2, 1, 0), heads)

        @pl.when(jnp.logical_not(late))
        def _():
            pl.semaphore_wait(barrier, 2 * late_low - 1)
            send_quarters((0, 1, 2), heads)

    for p in range(SUB // 2, pairs):
        transform(p)
    for j in range(m_dev):
        for w in range(n_wide):
            send1[j * n_wide + w, 2] = rearranged(SUB, rest, j, w)
    in_copies = []
    for i, (src, dst) in enumerate(
        ((leg_hbm.at[x], leg_v), (mixr_hbm, mixr_v), (mixi_hbm, mixi_v), (gain_hbm, gain_v))
    ):
        copy = pltpu.make_async_copy(src, dst, in_sem.at[i])
        copy.start()
        in_copies.append(copy)
    own_copy.start()

    @pl.when(upper_half)
    def _():
        @pl.when(late)
        def _():
            send_quarters((3, 2, 1, 0), tails)

        @pl.when(jnp.logical_not(late))
        def _():
            send_quarters((0, 1, 2), tails)

    @pl.when(jnp.logical_not(upper_half))
    def _():
        pl.semaphore_wait(barrier, 2 * late_low - 1)
        send_quarters((2, 1, 0), whole)

    @pl.when(jnp.logical_not(late))
    def _():
        pl.semaphore_wait(ready, 1)
        send_quarter(3, whole)

    for start in range(0, lon_count, LANES):
        size = min(LANES, lon_count - start)
        tabt_ref[start:start + size, :] = jnp.transpose(
            tab[:, start:start + size].astype(jnp.float32)
        ).astype(jnp.bfloat16)
    for copy in in_copies:
        copy.wait()
    lat_count = n_wide * lat_dev
    slot = lax.broadcasted_iota(jnp.int32, (2 * half, lat_count), 0)
    lat = lax.broadcasted_iota(jnp.int32, (2 * half, lat_count), 1)
    local = slot % SUB
    device = jnp.where(slot < half, slot, slot - half) // SUB
    want = device * lat_dev + jnp.where(slot < half, local, SUB + local % rest)
    pick = (want == lat).astype(jnp.bfloat16)
    moved = jnp.dot(pick, leg_v[...], preferred_element_type=jnp.float32)
    lt[...] = moved.astype(jnp.bfloat16)
    lf[...] = jnp.transpose(moved).astype(jnp.bfloat16)
    for i, who in enumerate((x, partner)):
        in_rows = pl.ds(pl.multiple_of(who * chan, chan), chan)
        for o in range(m_dev):
            re = mixr_v[in_rows, o * chan:(o + 1) * chan]
            im = mixi_v[in_rows, o * chan:(o + 1) * chan]
            top, left = 2 * i * chan, 2 * o * chan
            weight[top:top + chan, left:left + chan] = re
            weight[top:top + chan, left + chan:left + 2 * chan] = im
            weight[top + chan:top + 2 * chan, left:left + chan] = -im
            weight[top + chan:top + 2 * chan, left + chan:left + 2 * chan] = re

    def all_arrived(buf, count, sem):
        piece = buf.at[pl.ds(0, count)]
        pltpu.make_async_copy(piece, piece, sem).wait()

    tail_row = lax.broadcasted_iota(jnp.int32, (half, chan), 0) % SUB
    upper = tail_row < rest

    def analysed(who):
        from_there = pl.ds(who * n_wide, n_wide)
        tail = recv1[from_there, 2].reshape(half, chan)
        columns = []
        for ri in range(2):
            head = recv1[from_there, ri].reshape(half, chan)
            keep = upper if ri == 0 else jnp.logical_not(upper)
            columns.append(
                jnp.concatenate([head, jnp.where(keep, tail, jnp.zeros_like(tail))], axis=0)
            )
        spec = jnp.concatenate(columns, axis=1)
        return jnp.dot(lf[...], spec, preferred_element_type=jnp.float32).astype(jnp.bfloat16)

    own_copy.wait()
    all_arrived(recv1, n_wide - 1, s_recv.at[0])
    coeffs = analysed(x)
    partial[...] = jnp.dot(coeffs, weight[:2 * chan], preferred_element_type=jnp.float32)
    all_arrived(recv1, n_wide, s_recv.at[1])
    coeffs = analysed(partner)

    def back_copy(to):
        return pltpu.make_async_remote_copy(
            src_ref=send2.at[to[1] * n_wide + to[0]],
            dst_ref=recv2.at[x * n_wide + me],
            send_sem=b_send,
            recv_sem=b_recv.at[x],
            device_id=to,
            device_id_type=MESH,
        )

    lead = range(first)
    order = [[(w, 0) for w in lead], [(w, 1) for w in lead]]
    order[1] += [(w, side) for w in range(first, n_wide) for side in (0, 1)]
    for o in range(m_dev):
        cols = pl.ds(2 * o * chan, 2 * chan)
        product = partial[:, cols] + jnp.dot(
            coeffs, weight[2 * chan:, cols], preferred_element_type=jnp.float32
        )
        gain = gain_v[:, o * chan:(o + 1) * chan].astype(jnp.float32)
        gain = jnp.concatenate([gain, gain], axis=1)
        mixed[o] = (product * gain).astype(jnp.bfloat16)
        syn = jnp.dot(lt[...], mixed[o], preferred_element_type=jnp.float32)
        re, im = syn[:, :chan], syn[:, chan:]
        mine = pl.ds(o * n_wide, n_wide)
        tail = jnp.where(upper, re[half:], im[half:])
        for t, tile in enumerate((re[:half], im[:half], tail)):
            send2[mine, t] = tile.astype(jnp.bfloat16).reshape(n_wide, SUB, chan)
        for w, side in order[o]:
            @pl.when((w != me) | (side != x))
            def _():
                back_copy((w, side)).start()

    mine = x * n_wide + me
    own_back = pltpu.make_async_copy(send2.at[mine], recv2.at[mine], local_sem.at[1])
    own_back.start()
    all_arrived(send1, n_wide - 1, s_send.at[0])
    all_arrived(send1, n_wide, s_send.at[1])
    own_back.wait()
    for who in (x, partner):
        all_arrived(recv2, n_wide - 1 if who is x else n_wide, b_recv.at[who])
        flat2[...] = recv2[pl.ds(who * n_wide, n_wide)].astype(jnp.float32).reshape(
            n_wide * 3 * SUB, chan
        )
        for a in range(lat_dev):
            for ri in range(2):
                at = ri * SUB + a if a < SUB else 2 * SUB + ri * rest + a - SUB
                top = pl.multiple_of(row_of(who, ri, 0), n_wide)
                out_ref[a, pl.ds(top, n_wide), :] = flat2[
                    pl.ds(at, n_wide, stride=3 * SUB), :
                ].astype(jnp.bfloat16)
    all_arrived(send2, others, b_send)


def field_kernel(scale, tile, tabt_ref, syn_ref, out_hbm, held, sem):
    lat_dev, lon_count, chan = held.shape
    copies = []
    for a in range(0, lat_dev, 2):
        rhs = jnp.concatenate([syn_ref[a], syn_ref[a + 1]], axis=1)
        for i, start in enumerate(range(0, lon_count, tile)):
            here = slice(start, start + tile)
            res = jnp.dot(tabt_ref[here], rhs, preferred_element_type=jnp.float32) * scale
            res = res.astype(jnp.bfloat16)
            held[a, here] = res[:, :chan]
            held[a + 1, here] = res[:, chan:]
            if i % 2:
                done = (pl.ds(a, 2), pl.ds(start - tile, 2 * tile))
                copy = pltpu.make_async_copy(
                    held.at[done], out_hbm.at[done], sem.at[len(copies)]
                )
                copy.start()
                copies.append(copy)
    for copy in copies:
        copy.wait()


def fast_shards(grid, quad_weights, orders, legendre, mix_real, mix_imag, filter_gain):
    lat_dev, chan, lon_count = grid.shape
    order_count = orders.shape[0]
    m_dev, deg_count, lat_count = legendre.shape
    n_wide = lax.axis_size("wide")
    rows = 2 * order_count
    half = n_wide * SUB
    bf16, f32 = jnp.bfloat16, jnp.float32
    vmem = pl.BlockSpec(memory_space=pltpu.VMEM)
    hbm = pl.BlockSpec(memory_space=pltpu.HBM)
    dims = (n_wide, lat_dev, lon_count, chan, m_dev, deg_count)
    chan_all = mix_real.shape[0]
    dma = pltpu.SemaphoreType.DMA
    synthesis, table = pl.pallas_call(
        functools.partial(spectral_kernel, dims),
        out_shape=(
            jax.ShapeDtypeStruct((lat_dev, rows, chan), bf16),
            jax.ShapeDtypeStruct((lon_count, rows), bf16),
        ),
        in_specs=[hbm] * 7,
        out_specs=(vmem, vmem),
        scratch_shapes=[
            pltpu.VMEM((lat_dev, lon_count, chan), bf16),
            pltpu.VMEM((lat_count, deg_count), bf16),
            pltpu.VMEM((chan_all, chan_all), bf16),
            pltpu.VMEM((chan_all, chan_all), bf16),
            pltpu.VMEM((deg_count, chan_all), bf16),
            pltpu.VMEM((rows, lon_count), bf16),
            pltpu.VMEM((lat_dev * rows, chan), f32),
            pltpu.VMEM((order_count, 3, SUB, chan), bf16),
            pltpu.VMEM((order_count, 3, SUB, chan), bf16),
            pltpu.VMEM((2 * half, deg_count), bf16),
            pltpu.VMEM((deg_count, 2 * half), bf16),
            pltpu.VMEM((4 * chan, 4 * chan), bf16),
            pltpu.VMEM((deg_count, 4 * chan), f32),
            pltpu.VMEM((m_dev, deg_count, 2 * chan), bf16),
            pltpu.VMEM((order_count, 3, SUB, chan), bf16),
            pltpu.VMEM((order_count, 3, SUB, chan), bf16),
            pltpu.VMEM((n_wide * 3 * SUB, chan), f32),
            pltpu.SMEM((order_count,), jnp.int32),
            pltpu.SMEM((lat_dev,), f32),
            dma((lat_dev // 2,)),
            dma((6,)),
            dma((2,)),
            dma((2,)),
            dma((2,)),
            dma,
            dma((2,)),
            pltpu.SemaphoreType.REGULAR,
        ],
        compiler_params=pltpu.CompilerParams(
            collective_id=0, has_side_effects=True, vmem_limit_bytes=40 * 2**20
        ),
        name="spectral",
    )(*(pltpu.with_memory_space_constraint(v, pltpu.HBM) for v in (
        orders, quad_weights, jnp.transpose(grid, (0, 2, 1)), jnp.transpose(legendre, (0, 2, 1)),
        mix_real, mix_imag, filter_gain,
    )))
    field = pl.pallas_call(
        functools.partial(field_kernel, 1.0 / math.sqrt(order_count), lon_count // 6),
        out_shape=jax.ShapeDtypeStruct((lat_dev, lon_count, chan), bf16),
        in_specs=[vmem, vmem],
        out_specs=pl.BlockSpec(memory_space=pl.ANY),
        scratch_shapes=[pltpu.VMEM((lat_dev, lon_count, chan), bf16), dma((3 * lat_dev // 2,))],
        compiler_params=pltpu.CompilerParams(vmem_limit_bytes=24 * 2**20),
        name="field",
    )(table, synthesis)
    return jnp.transpose(field, (0, 2, 1))


def shards(grid, quad_weights, orders, legendre, mix_real, mix_imag, filter_gain):
    lat_dev, chan, lon_count = grid.shape
    m_dev = legendre.shape[0]
    n_wide = lax.axis_size("wide")
    rest = lat_dev - SUB
    fits = (
        lax.axis_size("narrow") == 2
        and chan == LANES
        and lon_count % 96 == 0
        and m_dev == 2
        and 2 * rest == SUB
        and lat_dev % 2 == 0
        and n_wide % 16 == 0
        and n_wide & (n_wide - 1) == 0
        and lon_count * lon_count < 2**24
    )
    body = fast_shards if fits else general_shards
    return body(grid, quad_weights, orders, legendre, mix_real, mix_imag, filter_gain)


def solution(mesh):
    placed = (P("wide", "narrow", None), P("wide"), P(), P("wide", None, None), P(), P(), P())
    return jax.shard_map(
        shards, mesh=mesh, in_specs=placed, out_specs=P("wide", "narrow", None), check_vma=False
    )
```

```python
import functools
import math

import jax
import jax.numpy as jnp
from jax import lax
from jax.experimental import pallas as pl
from jax.experimental.pallas import tpu as pltpu
from jax.sharding import PartitionSpec as P

MESH = pl.DeviceIdType.MESH
SUB = 8
LANES = 128


def fourier_tables(orders, lon_count):
    columns = jnp.arange(lon_count, dtype=jnp.int32)
    phase_int = orders[:, None] * columns[None, :] % lon_count
    angles = phase_int.astype(jnp.float32) * (2.0 * math.pi / lon_count)
    return (jnp.cos(angles).astype(jnp.bfloat16), jnp.sin(angles).astype(jnp.bfloat16))


def general_shards(grid, quad_weights, orders, legendre, mix_real, mix_imag, filter_gain):
    lon_count = grid.shape[2]
    order_count = orders.shape[0]
    cosine_table, sine_table = fourier_tables(orders, lon_count)
    factor = 1.0 / math.sqrt(lon_count)
    real_part = (
        jnp.einsum("acn,kn->kac", grid, cosine_table, preferred_element_type=jnp.float32) * factor
    )
    imag_part = (
        -jnp.einsum("acn,kn->kac", grid, sine_table, preferred_element_type=jnp.float32) * factor
    )
    spectra = (
        jnp.stack([real_part, imag_part], axis=2) * quad_weights[None, :, None, None]
    ).astype(jnp.bfloat16)
    by_order = lax.all_to_all(spectra, "wide", split_axis=0, concat_axis=1, tiled=True)
    m_dev = by_order.shape[0]
    lat_count = by_order.shape[1]
    chan_dev = by_order.shape[3]
    deg_count = legendre.shape[1]
    coeffs = jnp.einsum(
        "mlx,mxk->mlk",
        legendre,
        by_order.reshape(m_dev, lat_count, 2 * chan_dev),
        preferred_element_type=jnp.float32,
    )
    coeffs = coeffs.astype(jnp.bfloat16).reshape(m_dev, deg_count, 2, chan_dev)
    deg_dev = deg_count // lax.axis_size("narrow")
    gain_rows = lax.dynamic_slice_in_dim(
        filter_gain, lax.axis_index("narrow") * deg_dev, deg_dev, 0
    ).astype(jnp.float32)
    upper = jnp.concatenate([mix_real, mix_imag], axis=1)
    lower = jnp.concatenate([-mix_imag, mix_real], axis=1)
    wide_block = jnp.concatenate([upper, lower], axis=0)
    fragment = lax.all_to_all(coeffs, "narrow", split_axis=1, concat_axis=3, tiled=True)
    frag_count = fragment.shape[0]
    chan_all = fragment.shape[3]
    flat_rows = fragment.reshape(frag_count * deg_dev, 2 * chan_all)
    product = jnp.dot(flat_rows, wide_block, preferred_element_type=jnp.float32)
    product = product.reshape(frag_count, deg_dev, 2, chan_all) * gain_rows[None, :, None, :]
    mixed_coeffs = product.astype(jnp.bfloat16)
    back_coeffs = lax.all_to_all(mixed_coeffs, "narrow", split_axis=3, concat_axis=1, tiled=True)
    synthesis = jnp.einsum(
        "mlx,mlk->mxk",
        legendre,
        back_coeffs.reshape(m_dev, deg_count, 2 * chan_dev),
        preferred_element_type=jnp.float32,
    )
    synthesis = synthesis.astype(jnp.bfloat16).reshape(m_dev, lat_count, 2, chan_dev)
    by_latitude = lax.all_to_all(synthesis, "wide", split_axis=1, concat_axis=0, tiled=True)
    field_out = jnp.einsum(
        "kac,kn->acn", by_latitude[:, :, 0], cosine_table, preferred_element_type=jnp.float32
    )
    field_out = field_out - jnp.einsum(
        "kac,kn->acn", by_latitude[:, :, 1], sine_table, preferred_element_type=jnp.float32
    )
    return (field_out / math.sqrt(order_count)).astype(jnp.bfloat16)


def turn_both(phase, period):
    quarter = period // 4
    turns = jnp.floor(phase * (1.0 / quarter) + 0.5)
    angle = (phase - turns * quarter) * (2.0 * math.pi / period)
    quadrant = turns - 4.0 * jnp.floor(turns * 0.25)
    sq = angle * angle
    cosine = 1.0 + sq * (-0.5 + sq * (1.0 / 24 + sq * (-1.0 / 720 + sq * (1.0 / 40320))))
    sine = angle * (1.0 + sq * (-1.0 / 6 + sq * (1.0 / 120 + sq * (-1.0 / 5040 + sq * (1.0 / 362880)))))
    odd = (quadrant == 1.0) | (quadrant == 3.0)
    first = jnp.where(odd, sine, cosine)
    second = jnp.where(odd, cosine, sine)
    first = jnp.where((quadrant == 1.0) | (quadrant == 2.0), -first, first)
    second = jnp.where(quadrant >= 2.0, -second, second)
    return first, second


def rotate(pair, by):
    return pair[0] * by[0] - pair[1] * by[1], pair[1] * by[0] + pair[0] * by[1]


def spectral_kernel(
    dims, orders_hbm, quad_hbm, grid_hbm, leg_hbm, mixr_hbm, mixi_hbm, gain_hbm,
    out_ref, tabt_ref,
    grid_v, leg_v, mixr_v, mixi_v, gain_v, tab, spread, send1, recv1, lt, lf,
    weight, blend, mixed, send2, recv2, flat2, orders_ref, quad_ref,
    grid_sem, in_sem, local_sem, s_send, s_recv, b_send, b_recv, ready,
):
    n_wide, lat_dev, lon_count, chan, m_dev, deg_count = dims
    order_count = n_wide * m_dev
    rows = 2 * order_count
    rest = lat_dev - SUB
    hw = n_wide // 2
    hs = hw * SUB
    pairs = lat_dev // 2
    others = m_dev * n_wide - 1
    me = lax.axis_index("wide")
    x = lax.axis_index("narrow")

    steps = []
    bit = 1
    while bit < n_wide:
        steps.append(bit * (1 - 2 * (me // bit % 2)))
        bit *= 2

    def flipped(d):
        return me + functools.reduce(
            lambda a, b: a + b, [s for i, s in enumerate(steps) if d >> i & 1], 0
        )

    partner = 1 - x
    across = [(flipped(d), partner) for d in reversed(range(n_wide))]
    along = [(flipped(d), x) for d in reversed(range(1, n_wide))]

    scalar_copies = []
    for i, (src, dst) in enumerate(((orders_hbm, orders_ref), (quad_hbm, quad_ref))):
        copy = pltpu.make_async_copy(src, dst, in_sem.at[4 + i])
        copy.start()
        scalar_copies.append(copy)
    grid_copies = []
    for p in range(pairs):
        copy = pltpu.make_async_copy(
            grid_hbm.at[pl.ds(2 * p, 2)], grid_v.at[pl.ds(2 * p, 2)], grid_sem.at[p]
        )
        copy.start()
        grid_copies.append(copy)

    late_low = n_wide - n_wide // 4
    late = me >= late_low
    barrier = pltpu.get_barrier_semaphore()

    @pl.when(jnp.logical_not(late))
    def _():
        for d in range(n_wide):
            for to in across[d:d + 1] + along[d:d + 1]:
                pl.semaphore_signal(barrier, inc=1, device_id=to, device_id_type=MESH)

    @pl.when(late)
    def _():
        for d in reversed(range(n_wide // 4)):
            for to in (flipped(d), partner), (flipped(d), x):
                if d or to[1] is partner:
                    pl.semaphore_signal(barrier, inc=1, device_id=to, device_id_type=MESH)

    for copy in scalar_copies:
        copy.wait()
    block_rows = 2 * n_wide
    sub = lax.broadcasted_iota(jnp.int32, (SUB, LANES), 0)
    pieces = []
    for j in range(m_dev):
        for low in range(0, n_wide, SUB):
            piece = jnp.zeros((SUB, LANES), jnp.int32)
            for i in range(SUB):
                piece = jnp.where(sub == i, orders_ref[(low + i) * m_dev + j], piece)
            pieces.append(piece)
    order_row = jnp.concatenate(pieces, axis=0)
    lane = lax.broadcasted_iota(jnp.int32, (order_count, LANES), 1)
    group = 4
    block = turn_both((order_row * lane).astype(jnp.float32), lon_count)
    one = turn_both((order_row * LANES).astype(jnp.float32), lon_count)
    far = turn_both((order_row * (group * LANES)).astype(jnp.float32), lon_count)
    for i, start in enumerate(range(0, lon_count, LANES)):
        size = min(LANES, lon_count - start)
        if i % group == 0:
            block = block if i == 0 else rotate(block, far)
            now = block
        else:
            now = rotate(now, one)
        for j in range(m_dev):
            here = slice(j * n_wide, (j + 1) * n_wide)
            top = j * block_rows
            tab[top:top + n_wide, start:start + size] = now[0][here, :size].astype(jnp.bfloat16)
            tab[top + n_wide:top + block_rows, start:start + size] = (
                -now[1][here, :size]
            ).astype(jnp.bfloat16)

    @pl.when(late)
    def _():
        pl.semaphore_wait(barrier, others)
        for w in range(3):
            pl.semaphore_signal(
                ready, inc=1, device_id=(w * (n_wide // 4) + me % (n_wide // 4), x),
                device_id_type=MESH,
            )

    factor = 1.0 / math.sqrt(lon_count)

    def transform(p):
        grid_copies[p].wait()
        rhs = jnp.concatenate([grid_v[2 * p], grid_v[2 * p + 1]], axis=1)
        res = jnp.dot(tab[...], rhs, preferred_element_type=jnp.float32)
        for i in range(2):
            a = 2 * p + i
            spread[a * rows:(a + 1) * rows, :] = res[:, i * chan:(i + 1) * chan] * (
                quad_ref[a] * factor
            )

    def row_of(j, ri, w):
        return j * block_rows + ri * n_wide + w

    whole, heads, tails = pl.ds(0, 3), pl.ds(0, 2), pl.ds(2, 1)

    def out_copy(part, to, where):
        return pltpu.make_async_remote_copy(
            src_ref=send1.at[to[1] * n_wide + to[0], where],
            dst_ref=recv1.at[x * n_wide + me, where],
            send_sem=s_send.at[part],
            recv_sem=s_recv.at[part],
            device_id=to,
            device_id_type=MESH,
        )

    mine = x * n_wide + me
    own_copy = pltpu.make_async_copy(send1.at[mine], recv1.at[mine], local_sem.at[0])

    def rearranged(a, count, j, w):
        first = a * rows
        return jnp.concatenate(
            [
                spread[pl.ds(first + row_of(j, ri, w), count, stride=rows), :]
                for ri in range(2)
            ],
            axis=0,
        ).astype(jnp.bfloat16)

    chunk = n_wide // 4
    lower = (me < n_wide // 2).astype(jnp.int32)

    first = 2

    def send_first(where):
        for w in range(first):
            @pl.when((w != me) | (x > 0))
            def _():
                out_copy(1 - lower, (w, 0), where).start()

    def send_quarter(q, where):
        part = 1 - lower if q < 2 else lower
        for i, side in enumerate((x, partner)):
            for w in reversed(range(q * chunk, (q + 1) * chunk)):
                wanted = (w != me) | (i > 0)
                if w < first:
                    wanted = wanted & (side > 0)

                @pl.when(wanted)
                def _():
                    out_copy(part, (w, side), where).start()

    def send_quarters(order, where):
        send_first(where)
        for q in order:
            send_quarter(q, where)

    for p in range(SUB // 2):
        transform(p)
    for j in range(m_dev):
        for w in range(n_wide):
            send1[j * n_wide + w, :2] = rearranged(0, SUB, j, w).reshape(2, SUB, chan)
    upper_half = me >= n_wide // 2

    @pl.when(upper_half)
    def _():
        @pl.when(late)
        def _():
            send_quarters((3, 2, 1, 0), heads)

        @pl.when(jnp.logical_not(late))
        def _():
            pl.semaphore_wait(barrier, 2 * late_low - 1)
            send_quarters((0, 1, 2), heads)

    for p in range(SUB // 2, pairs):
        transform(p)
    for j in range(m_dev):
        for w in range(n_wide):
            send1[j * n_wide + w, 2] = rearranged(SUB, rest, j, w)
    in_copies = []
    for i, (src, dst) in enumerate(
        ((leg_hbm.at[x], leg_v), (mixr_hbm, mixr_v), (mixi_hbm, mixi_v), (gain_hbm, gain_v))
    ):
        copy = pltpu.make_async_copy(src, dst, in_sem.at[i])
        copy.start()
        in_copies.append(copy)
    own_copy.start()

    @pl.when(upper_half)
    def _():
        @pl.when(late)
        def _():
            send_quarters((3, 2, 1, 0), tails)

        @pl.when(jnp.logical_not(late))
        def _():
            send_quarters((0, 1, 2), tails)

    @pl.when(jnp.logical_not(upper_half))
    def _():
        pl.semaphore_wait(barrier, 2 * late_low - 1)
        send_quarters((2, 1, 0), whole)

    @pl.when(jnp.logical_not(late))
    def _():
        pl.semaphore_wait(ready, 1)
        send_quarter(3, whole)

    for start in range(0, lon_count, LANES):
        size = min(LANES, lon_count - start)
        tabt_ref[start:start + size, :] = jnp.transpose(
            tab[:, start:start + size].astype(jnp.float32)
        ).astype(jnp.bfloat16)
    for copy in in_copies:
        copy.wait()
    lat_count = n_wide * lat_dev
    slot = lax.broadcasted_iota(jnp.int32, (4 * hs, lat_count), 0)
    lat = lax.broadcasted_iota(jnp.int32, (4 * hs, lat_count), 1)
    local = slot % SUB
    device = slot // (2 * hs) * hw + slot % hs // SUB
    head = slot % (2 * hs) < hs
    want = device * lat_dev + jnp.where(head, local, SUB + local % rest)
    pick = (want == lat).astype(jnp.bfloat16)
    moved = jnp.dot(pick, leg_v[...], preferred_element_type=jnp.float32)
    lt[...] = moved.astype(jnp.bfloat16)
    lf[...] = jnp.transpose(moved).astype(jnp.bfloat16)
    for i in range(m_dev):
        in_rows = slice(i * chan, (i + 1) * chan)
        for o in range(m_dev):
            re = mixr_v[in_rows, o * chan:(o + 1) * chan]
            im = mixi_v[in_rows, o * chan:(o + 1) * chan]
            top, left = 2 * i * chan, 2 * o * chan
            weight[top:top + chan, left:left + chan] = re
            weight[top:top + chan, left + chan:left + 2 * chan] = im
            weight[top + chan:top + 2 * chan, left:left + chan] = -im
            weight[top + chan:top + 2 * chan, left + chan:left + 2 * chan] = re

    def all_arrived(buf, count, sem):
        piece = buf.at[pl.ds(0, count)]
        pltpu.make_async_copy(piece, piece, sem).wait()

    tail_row = lax.broadcasted_iota(jnp.int32, (hs, chan), 0) % SUB
    upper = tail_row < rest

    def spectra_from(h):
        heads_of, tails_of = [], []
        for i in range(m_dev):
            there = pl.ds(i * n_wide + h * hw, hw)
            tail = recv1[there, 2].reshape(hs, chan)
            for ri in range(2):
                heads_of.append(recv1[there, ri].reshape(hs, chan))
                keep = upper if ri == 0 else jnp.logical_not(upper)
                tails_of.append(jnp.where(keep, tail, jnp.zeros_like(tail)))
        return jnp.concatenate(
            [jnp.concatenate(heads_of, axis=1), jnp.concatenate(tails_of, axis=1)], axis=0
        )

    def rows_from(h):
        return pl.ds(pl.multiple_of(h * 2 * hs, 2 * hs), 2 * hs)

    here, there = 1 - lower, lower
    own_copy.wait()
    all_arrived(recv1, n_wide - 1, s_recv.at[0])
    blend[rows_from(here), :] = jnp.dot(
        spectra_from(here), weight[...], preferred_element_type=jnp.float32
    ).astype(jnp.bfloat16)
    all_arrived(recv1, n_wide, s_recv.at[1])
    spec = spectra_from(there)

    def back_copy(to):
        return pltpu.make_async_remote_copy(
            src_ref=send2.at[to[1] * n_wide + to[0]],
            dst_ref=recv2.at[x * n_wide + me],
            send_sem=b_send,
            recv_sem=b_recv.at[x],
            device_id=to,
            device_id_type=MESH,
        )

    lead = range(first)
    order = [[(w, 0) for w in lead], [(w, 1) for w in lead]]
    order[1] += [(w, side) for w in range(first, n_wide) for side in (0, 1)]
    for o in range(m_dev):
        cols = pl.ds(2 * o * chan, 2 * chan)
        blend[rows_from(there), cols] = jnp.dot(
            spec, weight[:, cols], preferred_element_type=jnp.float32
        ).astype(jnp.bfloat16)
        product = jnp.dot(lf[...], blend[:, cols], preferred_element_type=jnp.float32)
        gain = gain_v[:, o * chan:(o + 1) * chan].astype(jnp.float32)
        gain = jnp.concatenate([gain, gain], axis=1)
        mixed[o] = (product * gain).astype(jnp.bfloat16)
        syn = jnp.dot(lt[...], mixed[o], preferred_element_type=jnp.float32)
        for h in range(2):
            block = syn[h * 2 * hs:(h + 1) * 2 * hs]
            re, im = block[:, :chan], block[:, chan:]
            tail = jnp.where(upper, re[hs:], im[hs:])
            for t, tile in enumerate((re[:hs], im[:hs], tail)):
                send2[pl.ds(o * n_wide + h * hw, hw), t] = tile.astype(jnp.bfloat16).reshape(
                    hw, SUB, chan
                )
        for w, side in order[o]:
            @pl.when((w != me) | (side != x))
            def _():
                back_copy((w, side)).start()

    mine = x * n_wide + me
    own_back = pltpu.make_async_copy(send2.at[mine], recv2.at[mine], local_sem.at[1])
    own_back.start()
    all_arrived(send1, n_wide - 1, s_send.at[0])
    all_arrived(send1, n_wide, s_send.at[1])
    own_back.wait()
    for who in (x, partner):
        all_arrived(recv2, n_wide - 1 if who is x else n_wide, b_recv.at[who])
        flat2[...] = recv2[pl.ds(who * n_wide, n_wide)].astype(jnp.float32).reshape(
            n_wide * 3 * SUB, chan
        )
        for a in range(lat_dev):
            for ri in range(2):
                at = ri * SUB + a if a < SUB else 2 * SUB + ri * rest + a - SUB
                top = pl.multiple_of(row_of(who, ri, 0), n_wide)
                out_ref[a, pl.ds(top, n_wide), :] = flat2[
                    pl.ds(at, n_wide, stride=3 * SUB), :
                ].astype(jnp.bfloat16)
    all_arrived(send2, others, b_send)


def field_kernel(scale, tile, tabt_ref, syn_ref, out_hbm, held, sem):
    lat_dev, lon_count, chan = held.shape
    copies = []
    for a in range(0, lat_dev, 2):
        rhs = jnp.concatenate([syn_ref[a], syn_ref[a + 1]], axis=1)
        for i, start in enumerate(range(0, lon_count, tile)):
            here = slice(start, start + tile)
            res = jnp.dot(tabt_ref[here], rhs, preferred_element_type=jnp.float32) * scale
            res = res.astype(jnp.bfloat16)
            held[a, here] = res[:, :chan]
            held[a + 1, here] = res[:, chan:]
            if i % 2:
                done = (pl.ds(a, 2), pl.ds(start - tile, 2 * tile))
                copy = pltpu.make_async_copy(
                    held.at[done], out_hbm.at[done], sem.at[len(copies)]
                )
                copy.start()
                copies.append(copy)
    for copy in copies:
        copy.wait()


def fast_shards(grid, quad_weights, orders, legendre, mix_real, mix_imag, filter_gain):
    lat_dev, chan, lon_count = grid.shape
    order_count = orders.shape[0]
    m_dev, deg_count, lat_count = legendre.shape
    n_wide = lax.axis_size("wide")
    rows = 2 * order_count
    half = n_wide * SUB
    bf16, f32 = jnp.bfloat16, jnp.float32
    vmem = pl.BlockSpec(memory_space=pltpu.VMEM)
    hbm = pl.BlockSpec(memory_space=pltpu.HBM)
    dims = (n_wide, lat_dev, lon_count, chan, m_dev, deg_count)
    chan_all = mix_real.shape[0]
    dma = pltpu.SemaphoreType.DMA
    synthesis, table = pl.pallas_call(
        functools.partial(spectral_kernel, dims),
        out_shape=(
            jax.ShapeDtypeStruct((lat_dev, rows, chan), bf16),
            jax.ShapeDtypeStruct((lon_count, rows), bf16),
        ),
        in_specs=[hbm] * 7,
        out_specs=(vmem, vmem),
        scratch_shapes=[
            pltpu.VMEM((lat_dev, lon_count, chan), bf16),
            pltpu.VMEM((lat_count, deg_count), bf16),
            pltpu.VMEM((chan_all, chan_all), bf16),
            pltpu.VMEM((chan_all, chan_all), bf16),
            pltpu.VMEM((deg_count, chan_all), bf16),
            pltpu.VMEM((rows, lon_count), bf16),
            pltpu.VMEM((lat_dev * rows, chan), f32),
            pltpu.VMEM((order_count, 3, SUB, chan), bf16),
            pltpu.VMEM((order_count, 3, SUB, chan), bf16),
            pltpu.VMEM((2 * half, deg_count), bf16),
            pltpu.VMEM((deg_count, 2 * half), bf16),
            pltpu.VMEM((4 * chan, 4 * chan), bf16),
            pltpu.VMEM((2 * half, 4 * chan), bf16),
            pltpu.VMEM((m_dev, deg_count, 2 * chan), bf16),
            pltpu.VMEM((order_count, 3, SUB, chan), bf16),
            pltpu.VMEM((order_count, 3, SUB, chan), bf16),
            pltpu.VMEM((n_wide * 3 * SUB, chan), f32),
            pltpu.SMEM((order_count,), jnp.int32),
            pltpu.SMEM((lat_dev,), f32),
            dma((lat_dev // 2,)),
            dma((6,)),
            dma((2,)),
            dma((2,)),
            dma((2,)),
            dma,
            dma((2,)),
            pltpu.SemaphoreType.REGULAR,
        ],
        compiler_params=pltpu.CompilerParams(
            collective_id=0, has_side_effects=True, vmem_limit_bytes=40 * 2**20
        ),
        name="spectral",
    )(*(pltpu.with_memory_space_constraint(v, pltpu.HBM) for v in (
        orders, quad_weights, jnp.transpose(grid, (0, 2, 1)), jnp.transpose(legendre, (0, 2, 1)),
        mix_real, mix_imag, filter_gain,
    )))
    field = pl.pallas_call(
        functools.partial(field_kernel, 1.0 / math.sqrt(order_count), lon_count // 6),
        out_shape=jax.ShapeDtypeStruct((lat_dev, lon_count, chan), bf16),
        in_specs=[vmem, vmem],
        out_specs=pl.BlockSpec(memory_space=pl.ANY),
        scratch_shapes=[pltpu.VMEM((lat_dev, lon_count, chan), bf16), dma((3 * lat_dev // 2,))],
        compiler_params=pltpu.CompilerParams(vmem_limit_bytes=24 * 2**20),
        name="field",
    )(table, synthesis)
    return jnp.transpose(field, (0, 2, 1))


def shards(grid, quad_weights, orders, legendre, mix_real, mix_imag, filter_gain):
    lat_dev, chan, lon_count = grid.shape
    m_dev = legendre.shape[0]
    n_wide = lax.axis_size("wide")
    rest = lat_dev - SUB
    fits = (
        lax.axis_size("narrow") == 2
        and chan == LANES
        and lon_count % 96 == 0
        and m_dev == 2
        and 2 * rest == SUB
        and lat_dev % 2 == 0
        and n_wide % 16 == 0
        and n_wide & (n_wide - 1) == 0
        and lon_count * lon_count < 2**24
    )
    body = fast_shards if fits else general_shards
    return body(grid, quad_weights, orders, legendre, mix_real, mix_imag, filter_gain)


def solution(mesh):
    placed = (P("wide", "narrow", None), P("wide"), P(), P("wide", None, None), P(), P(), P())
    return jax.shard_map(
        shards, mesh=mesh, in_specs=placed, out_specs=P("wide", "narrow", None), check_vma=False
    )
```

```python
import functools
import math

import jax
import jax.numpy as jnp
from jax import lax
from jax.experimental import pallas as pl
from jax.experimental.pallas import tpu as pltpu
from jax.sharding import PartitionSpec as P

MESH = pl.DeviceIdType.MESH
SUB = 8
LANES = 128


def fourier_tables(orders, lon_count):
    columns = jnp.arange(lon_count, dtype=jnp.int32)
    phase_int = orders[:, None] * columns[None, :] % lon_count
    angles = phase_int.astype(jnp.float32) * (2.0 * math.pi / lon_count)
    return (jnp.cos(angles).astype(jnp.bfloat16), jnp.sin(angles).astype(jnp.bfloat16))


def general_shards(grid, quad_weights, orders, legendre, mix_real, mix_imag, filter_gain):
    lon_count = grid.shape[2]
    order_count = orders.shape[0]
    cosine_table, sine_table = fourier_tables(orders, lon_count)
    factor = 1.0 / math.sqrt(lon_count)
    real_part = (
        jnp.einsum("acn,kn->kac", grid, cosine_table, preferred_element_type=jnp.float32) * factor
    )
    imag_part = (
        -jnp.einsum("acn,kn->kac", grid, sine_table, preferred_element_type=jnp.float32) * factor
    )
    spectra = (
        jnp.stack([real_part, imag_part], axis=2) * quad_weights[None, :, None, None]
    ).astype(jnp.bfloat16)
    by_order = lax.all_to_all(spectra, "wide", split_axis=0, concat_axis=1, tiled=True)
    m_dev = by_order.shape[0]
    lat_count = by_order.shape[1]
    chan_dev = by_order.shape[3]
    deg_count = legendre.shape[1]
    coeffs = jnp.einsum(
        "mlx,mxk->mlk",
        legendre,
        by_order.reshape(m_dev, lat_count, 2 * chan_dev),
        preferred_element_type=jnp.float32,
    )
    coeffs = coeffs.astype(jnp.bfloat16).reshape(m_dev, deg_count, 2, chan_dev)
    deg_dev = deg_count // lax.axis_size("narrow")
    gain_rows = lax.dynamic_slice_in_dim(
        filter_gain, lax.axis_index("narrow") * deg_dev, deg_dev, 0
    ).astype(jnp.float32)
    upper = jnp.concatenate([mix_real, mix_imag], axis=1)
    lower = jnp.concatenate([-mix_imag, mix_real], axis=1)
    wide_block = jnp.concatenate([upper, lower], axis=0)
    fragment = lax.all_to_all(coeffs, "narrow", split_axis=1, concat_axis=3, tiled=True)
    frag_count = fragment.shape[0]
    chan_all = fragment.shape[3]
    flat_rows = fragment.reshape(frag_count * deg_dev, 2 * chan_all)
    product = jnp.dot(flat_rows, wide_block, preferred_element_type=jnp.float32)
    product = product.reshape(frag_count, deg_dev, 2, chan_all) * gain_rows[None, :, None, :]
    mixed_coeffs = product.astype(jnp.bfloat16)
    back_coeffs = lax.all_to_all(mixed_coeffs, "narrow", split_axis=3, concat_axis=1, tiled=True)
    synthesis = jnp.einsum(
        "mlx,mlk->mxk",
        legendre,
        back_coeffs.reshape(m_dev, deg_count, 2 * chan_dev),
        preferred_element_type=jnp.float32,
    )
    synthesis = synthesis.astype(jnp.bfloat16).reshape(m_dev, lat_count, 2, chan_dev)
    by_latitude = lax.all_to_all(synthesis, "wide", split_axis=1, concat_axis=0, tiled=True)
    field_out = jnp.einsum(
        "kac,kn->acn", by_latitude[:, :, 0], cosine_table, preferred_element_type=jnp.float32
    )
    field_out = field_out - jnp.einsum(
        "kac,kn->acn", by_latitude[:, :, 1], sine_table, preferred_element_type=jnp.float32
    )
    return (field_out / math.sqrt(order_count)).astype(jnp.bfloat16)


def turn_both(phase, period):
    quarter = period // 4
    turns = jnp.floor(phase * (1.0 / quarter) + 0.5)
    angle = (phase - turns * quarter) * (2.0 * math.pi / period)
    quadrant = turns - 4.0 * jnp.floor(turns * 0.25)
    sq = angle * angle
    cosine = 1.0 + sq * (-0.5 + sq * (1.0 / 24 + sq * (-1.0 / 720 + sq * (1.0 / 40320))))
    sine = angle * (1.0 + sq * (-1.0 / 6 + sq * (1.0 / 120 + sq * (-1.0 / 5040 + sq * (1.0 / 362880)))))
    odd = (quadrant == 1.0) | (quadrant == 3.0)
    first = jnp.where(odd, sine, cosine)
    second = jnp.where(odd, cosine, sine)
    first = jnp.where((quadrant == 1.0) | (quadrant == 2.0), -first, first)
    second = jnp.where(quadrant >= 2.0, -second, second)
    return first, second


def rotate(pair, by):
    return pair[0] * by[0] - pair[1] * by[1], pair[1] * by[0] + pair[0] * by[1]


def spectral_kernel(
    dims, orders_hbm, quad_hbm, grid_hbm, leg_hbm, mixr_hbm, mixi_hbm, gain_hbm,
    out_ref, tabt_ref,
    grid_v, leg_v, mixr_v, mixi_v, gain_v, tab, spread, send1, recv1, lt, lf,
    weight, blend, mixed, send2, recv2, flat2, orders_ref, quad_ref,
    grid_sem, in_sem, local_sem, s_send, s_recv, b_send, b_recv, ready,
):
    n_wide, lat_dev, lon_count, chan, m_dev, deg_count = dims
    order_count = n_wide * m_dev
    rows = 2 * order_count
    rest = lat_dev - SUB
    hw = n_wide // 2
    hs = hw * SUB
    pairs = lat_dev // 2
    others = m_dev * n_wide - 1
    me = lax.axis_index("wide")
    x = lax.axis_index("narrow")

    steps = []
    bit = 1
    while bit < n_wide:
        steps.append(bit * (1 - 2 * (me // bit % 2)))
        bit *= 2

    def flipped(d):
        return me + functools.reduce(
            lambda a, b: a + b, [s for i, s in enumerate(steps) if d >> i & 1], 0
        )

    partner = 1 - x
    across = [(flipped(d), partner) for d in reversed(range(n_wide))]
    along = [(flipped(d), x) for d in reversed(range(1, n_wide))]

    scalar_copies = []
    for i, (src, dst) in enumerate(((orders_hbm, orders_ref), (quad_hbm, quad_ref))):
        copy = pltpu.make_async_copy(src, dst, in_sem.at[4 + i])
        copy.start()
        scalar_copies.append(copy)
    grid_copies = []
    for p in range(pairs):
        copy = pltpu.make_async_copy(
            grid_hbm.at[pl.ds(2 * p, 2)], grid_v.at[pl.ds(2 * p, 2)], grid_sem.at[p]
        )
        copy.start()
        grid_copies.append(copy)

    late_low = n_wide - n_wide // 4
    late = me >= late_low
    barrier = pltpu.get_barrier_semaphore()

    @pl.when(jnp.logical_not(late))
    def _():
        for d in range(n_wide):
            for to in across[d:d + 1] + along[d:d + 1]:
                pl.semaphore_signal(barrier, inc=1, device_id=to, device_id_type=MESH)

    @pl.when(late)
    def _():
        for d in reversed(range(n_wide // 4)):
            for to in (flipped(d), partner), (flipped(d), x):
                if d or to[1] is partner:
                    pl.semaphore_signal(barrier, inc=1, device_id=to, device_id_type=MESH)

    for copy in scalar_copies:
        copy.wait()
    block_rows = 2 * n_wide
    sub = lax.broadcasted_iota(jnp.int32, (SUB, LANES), 0)
    pieces = []
    for j in range(m_dev):
        for low in range(0, n_wide, SUB):
            piece = jnp.zeros((SUB, LANES), jnp.int32)
            for i in range(SUB):
                piece = jnp.where(sub == i, orders_ref[(low + i) * m_dev + j], piece)
            pieces.append(piece)
    order_row = jnp.concatenate(pieces, axis=0)
    lane = lax.broadcasted_iota(jnp.int32, (order_count, LANES), 1)
    group = 4
    block = turn_both((order_row * lane).astype(jnp.float32), lon_count)
    one = turn_both((order_row * LANES).astype(jnp.float32), lon_count)
    far = turn_both((order_row * (group * LANES)).astype(jnp.float32), lon_count)
    for i, start in enumerate(range(0, lon_count, LANES)):
        size = min(LANES, lon_count - start)
        if i % group == 0:
            block = block if i == 0 else rotate(block, far)
            now = block
        else:
            now = rotate(now, one)
        for j in range(m_dev):
            here = slice(j * n_wide, (j + 1) * n_wide)
            top = j * block_rows
            tab[top:top + n_wide, start:start + size] = now[0][here, :size].astype(jnp.bfloat16)
            tab[top + n_wide:top + block_rows, start:start + size] = (
                -now[1][here, :size]
            ).astype(jnp.bfloat16)

    @pl.when(late)
    def _():
        pl.semaphore_wait(barrier, others)
        for w in range(3):
            pl.semaphore_signal(
                ready, inc=1, device_id=(w * (n_wide // 4) + me % (n_wide // 4), x),
                device_id_type=MESH,
            )

    factor = 1.0 / math.sqrt(lon_count)

    def transform(p):
        grid_copies[p].wait()
        rhs = jnp.concatenate([grid_v[2 * p], grid_v[2 * p + 1]], axis=1)
        res = jnp.dot(tab[...], rhs, preferred_element_type=jnp.float32)
        for i in range(2):
            a = 2 * p + i
            spread[a * rows:(a + 1) * rows, :] = res[:, i * chan:(i + 1) * chan] * (
                quad_ref[a] * factor
            )

    def row_of(j, ri, w):
        return j * block_rows + ri * n_wide + w

    whole, heads, tails = pl.ds(0, 3), pl.ds(0, 2), pl.ds(2, 1)

    def out_copy(part, to, where):
        return pltpu.make_async_remote_copy(
            src_ref=send1.at[to[1] * n_wide + to[0], where],
            dst_ref=recv1.at[x * n_wide + me, where],
            send_sem=s_send.at[part],
            recv_sem=s_recv.at[part],
            device_id=to,
            device_id_type=MESH,
        )

    mine = x * n_wide + me
    own_copy = pltpu.make_async_copy(send1.at[mine], recv1.at[mine], local_sem.at[0])

    def rearranged(a, count, j, w):
        first = a * rows
        return jnp.concatenate(
            [
                spread[pl.ds(first + row_of(j, ri, w), count, stride=rows), :]
                for ri in range(2)
            ],
            axis=0,
        ).astype(jnp.bfloat16)

    chunk = n_wide // 4
    lower = (me < n_wide // 2).astype(jnp.int32)

    first = 2

    def send_first(where):
        for w in range(first):
            @pl.when((w != me) | (x > 0))
            def _():
                out_copy(1 - lower, (w, 0), where).start()

    def send_quarter(q, where):
        part = 1 - lower if q < 2 else lower
        for i, side in enumerate((x, partner)):
            for w in reversed(range(q * chunk, (q + 1) * chunk)):
                wanted = (w != me) | (i > 0)
                if w < first:
                    wanted = wanted & (side > 0)

                @pl.when(wanted)
                def _():
                    out_copy(part, (w, side), where).start()

    def send_quarters(order, where):
        send_first(where)
        for q in order:
            send_quarter(q, where)

    for p in range(SUB // 2):
        transform(p)
    for j in range(m_dev):
        for w in range(n_wide):
            send1[j * n_wide + w, :2] = rearranged(0, SUB, j, w).reshape(2, SUB, chan)
    upper_half = me >= n_wide // 2

    @pl.when(upper_half)
    def _():
        @pl.when(late)
        def _():
            send_quarters((3, 2, 1, 0), heads)

        @pl.when(jnp.logical_not(late))
        def _():
            pl.semaphore_wait(barrier, 2 * late_low - 1)
            send_quarters((0, 1, 2), heads)

    for p in range(SUB // 2, pairs):
        transform(p)
    for j in range(m_dev):
        for w in range(n_wide):
            send1[j * n_wide + w, 2] = rearranged(SUB, rest, j, w)
    in_copies = []
    for i, (src, dst) in enumerate(
        ((leg_hbm.at[x], leg_v), (mixr_hbm, mixr_v), (mixi_hbm, mixi_v), (gain_hbm, gain_v))
    ):
        copy = pltpu.make_async_copy(src, dst, in_sem.at[i])
        copy.start()
        in_copies.append(copy)
    own_copy.start()

    @pl.when(upper_half)
    def _():
        @pl.when(late)
        def _():
            send_quarters((3, 2, 1, 0), tails)

        @pl.when(jnp.logical_not(late))
        def _():
            send_quarters((0, 1, 2), tails)

    @pl.when(jnp.logical_not(upper_half))
    def _():
        pl.semaphore_wait(barrier, 2 * late_low - 1)
        send_quarters((2, 1, 0), whole)

    @pl.when(jnp.logical_not(late))
    def _():
        pl.semaphore_wait(ready, 1)
        send_quarter(3, whole)

    for start in range(0, lon_count, LANES):
        size = min(LANES, lon_count - start)
        tabt_ref[start:start + size, :] = jnp.transpose(
            tab[:, start:start + size].astype(jnp.float32)
        ).astype(jnp.bfloat16)
    for copy in in_copies:
        copy.wait()
    lat_count = n_wide * lat_dev
    slot = lax.broadcasted_iota(jnp.int32, (4 * hs, lat_count), 0)
    lat = lax.broadcasted_iota(jnp.int32, (4 * hs, lat_count), 1)
    local = slot % SUB
    device = slot // (2 * hs) * hw + slot % hs // SUB
    head = slot % (2 * hs) < hs
    want = device * lat_dev + jnp.where(head, local, SUB + local % rest)
    pick = (want == lat).astype(jnp.bfloat16)
    moved = jnp.dot(pick, leg_v[...], preferred_element_type=jnp.float32)
    lt[...] = moved.astype(jnp.bfloat16)
    lf[...] = jnp.transpose(moved).astype(jnp.bfloat16)
    for i in range(m_dev):
        in_rows = slice(i * chan, (i + 1) * chan)
        for o in range(m_dev):
            re = mixr_v[in_rows, o * chan:(o + 1) * chan]
            im = mixi_v[in_rows, o * chan:(o + 1) * chan]
            top, left = 2 * i * chan, 2 * o * chan
            weight[top:top + chan, left:left + chan] = re
            weight[top:top + chan, left + chan:left + 2 * chan] = im
            weight[top + chan:top + 2 * chan, left:left + chan] = -im
            weight[top + chan:top + 2 * chan, left + chan:left + 2 * chan] = re

    def all_arrived(buf, count, sem):
        piece = buf.at[pl.ds(0, count)]
        pltpu.make_async_copy(piece, piece, sem).wait()

    tail_row = lax.broadcasted_iota(jnp.int32, (hs, chan), 0) % SUB
    upper = tail_row < rest

    def spectra_from(h):
        heads_of, tails_of = [], []
        for i in range(m_dev):
            there = pl.ds(i * n_wide + h * hw, hw)
            tail = recv1[there, 2].reshape(hs, chan)
            for ri in range(2):
                heads_of.append(recv1[there, ri].reshape(hs, chan))
                keep = upper if ri == 0 else jnp.logical_not(upper)
                tails_of.append(jnp.where(keep, tail, jnp.zeros_like(tail)))
        return jnp.concatenate(
            [jnp.concatenate(heads_of, axis=1), jnp.concatenate(tails_of, axis=1)], axis=0
        )

    def rows_from(h):
        return pl.ds(pl.multiple_of(h * 2 * hs, 2 * hs), 2 * hs)

    here, there = 1 - lower, lower
    own_copy.wait()
    all_arrived(recv1, n_wide - 1, s_recv.at[0])
    blend[rows_from(here), :] = jnp.dot(
        spectra_from(here), weight[...], preferred_element_type=jnp.float32
    ).astype(jnp.bfloat16)
    all_arrived(recv1, n_wide, s_recv.at[1])
    spec = spectra_from(there)

    def back_copy(to):
        return pltpu.make_async_remote_copy(
            src_ref=send2.at[to[1] * n_wide + to[0]],
            dst_ref=recv2.at[x * n_wide + me],
            send_sem=b_send,
            recv_sem=b_recv.at[x],
            device_id=to,
            device_id_type=MESH,
        )

    lead = range(first)
    order = [[(w, 0) for w in lead], [(w, 1) for w in lead]]
    order[1] += [(w, side) for w in range(first, n_wide) for side in (0, 1)]
    blend[rows_from(there), :] = jnp.dot(
        spec, weight[...], preferred_element_type=jnp.float32
    ).astype(jnp.bfloat16)
    step = deg_count // 1
    for low in range(0, deg_count, step):
        part = slice(low, low + step)
        product = jnp.dot(lf[part], blend[...], preferred_element_type=jnp.float32)
        gain = gain_v[part].astype(jnp.float32)
        gain = jnp.concatenate(
            [gain[:, o * chan:(o + 1) * chan] for o in range(m_dev) for _ in range(2)], axis=1
        )
        mixed[part] = (product * gain).astype(jnp.bfloat16)
    for o in range(m_dev):
        syn = jnp.dot(
            lt[...], mixed[:, 2 * o * chan:2 * (o + 1) * chan],
            preferred_element_type=jnp.float32,
        )
        for h in range(2):
            block = syn[h * 2 * hs:(h + 1) * 2 * hs]
            re, im = block[:, :chan], block[:, chan:]
            tail = jnp.where(upper, re[hs:], im[hs:])
            for t, tile in enumerate((re[:hs], im[:hs], tail)):
                send2[pl.ds(o * n_wide + h * hw, hw), t] = tile.astype(jnp.bfloat16).reshape(
                    hw, SUB, chan
                )
    for w, side in order[0] + order[1]:
        @pl.when((w != me) | (side != x))
        def _():
            back_copy((w, side)).start()

    mine = x * n_wide + me
    own_back = pltpu.make_async_copy(send2.at[mine], recv2.at[mine], local_sem.at[1])
    own_back.start()
    all_arrived(send1, n_wide - 1, s_send.at[0])
    all_arrived(send1, n_wide, s_send.at[1])
    own_back.wait()
    for who in (x, partner):
        all_arrived(recv2, n_wide - 1 if who is x else n_wide, b_recv.at[who])
        flat2[...] = recv2[pl.ds(who * n_wide, n_wide)].astype(jnp.float32).reshape(
            n_wide * 3 * SUB, chan
        )
        for a in range(lat_dev):
            for ri in range(2):
                at = ri * SUB + a if a < SUB else 2 * SUB + ri * rest + a - SUB
                top = pl.multiple_of(row_of(who, ri, 0), n_wide)
                out_ref[a, pl.ds(top, n_wide), :] = flat2[
                    pl.ds(at, n_wide, stride=3 * SUB), :
                ].astype(jnp.bfloat16)
    all_arrived(send2, others, b_send)


def field_kernel(scale, tile, tabt_ref, syn_ref, out_hbm, held, sem):
    lat_dev, lon_count, chan = held.shape
    copies = []
    for a in range(0, lat_dev, 2):
        rhs = jnp.concatenate([syn_ref[a], syn_ref[a + 1]], axis=1)
        for i, start in enumerate(range(0, lon_count, tile)):
            here = slice(start, start + tile)
            res = jnp.dot(tabt_ref[here], rhs, preferred_element_type=jnp.float32) * scale
            res = res.astype(jnp.bfloat16)
            held[a, here] = res[:, :chan]
            held[a + 1, here] = res[:, chan:]
            if i % 2:
                done = (pl.ds(a, 2), pl.ds(start - tile, 2 * tile))
                copy = pltpu.make_async_copy(
                    held.at[done], out_hbm.at[done], sem.at[len(copies)]
                )
                copy.start()
                copies.append(copy)
    for copy in copies:
        copy.wait()


def fast_shards(grid, quad_weights, orders, legendre, mix_real, mix_imag, filter_gain):
    lat_dev, chan, lon_count = grid.shape
    order_count = orders.shape[0]
    m_dev, deg_count, lat_count = legendre.shape
    n_wide = lax.axis_size("wide")
    rows = 2 * order_count
    half = n_wide * SUB
    bf16, f32 = jnp.bfloat16, jnp.float32
    vmem = pl.BlockSpec(memory_space=pltpu.VMEM)
    hbm = pl.BlockSpec(memory_space=pltpu.HBM)
    dims = (n_wide, lat_dev, lon_count, chan, m_dev, deg_count)
    chan_all = mix_real.shape[0]
    dma = pltpu.SemaphoreType.DMA
    synthesis, table = pl.pallas_call(
        functools.partial(spectral_kernel, dims),
        out_shape=(
            jax.ShapeDtypeStruct((lat_dev, rows, chan), bf16),
            jax.ShapeDtypeStruct((lon_count, rows), bf16),
        ),
        in_specs=[hbm] * 7,
        out_specs=(vmem, vmem),
        scratch_shapes=[
            pltpu.VMEM((lat_dev, lon_count, chan), bf16),
            pltpu.VMEM((lat_count, deg_count), bf16),
            pltpu.VMEM((chan_all, chan_all), bf16),
            pltpu.VMEM((chan_all, chan_all), bf16),
            pltpu.VMEM((deg_count, chan_all), bf16),
            pltpu.VMEM((rows, lon_count), bf16),
            pltpu.VMEM((lat_dev * rows, chan), f32),
            pltpu.VMEM((order_count, 3, SUB, chan), bf16),
            pltpu.VMEM((order_count, 3, SUB, chan), bf16),
            pltpu.VMEM((2 * half, deg_count), bf16),
            pltpu.VMEM((deg_count, 2 * half), bf16),
            pltpu.VMEM((4 * chan, 4 * chan), bf16),
            pltpu.VMEM((2 * half, 4 * chan), bf16),
            pltpu.VMEM((deg_count, 4 * chan), bf16),
            pltpu.VMEM((order_count, 3, SUB, chan), bf16),
            pltpu.VMEM((order_count, 3, SUB, chan), bf16),
            pltpu.VMEM((n_wide * 3 * SUB, chan), f32),
            pltpu.SMEM((order_count,), jnp.int32),
            pltpu.SMEM((lat_dev,), f32),
            dma((lat_dev // 2,)),
            dma((6,)),
            dma((2,)),
            dma((2,)),
            dma((2,)),
            dma,
            dma((2,)),
            pltpu.SemaphoreType.REGULAR,
        ],
        compiler_params=pltpu.CompilerParams(
            collective_id=0, has_side_effects=True, vmem_limit_bytes=40 * 2**20
        ),
        name="spectral",
    )(*(pltpu.with_memory_space_constraint(v, pltpu.HBM) for v in (
        orders, quad_weights, jnp.transpose(grid, (0, 2, 1)), jnp.transpose(legendre, (0, 2, 1)),
        mix_real, mix_imag, filter_gain,
    )))
    field = pl.pallas_call(
        functools.partial(field_kernel, 1.0 / math.sqrt(order_count), lon_count // 6),
        out_shape=jax.ShapeDtypeStruct((lat_dev, lon_count, chan), bf16),
        in_specs=[vmem, vmem],
        out_specs=pl.BlockSpec(memory_space=pl.ANY),
        scratch_shapes=[pltpu.VMEM((lat_dev, lon_count, chan), bf16), dma((3 * lat_dev // 2,))],
        compiler_params=pltpu.CompilerParams(vmem_limit_bytes=24 * 2**20),
        name="field",
    )(table, synthesis)
    return jnp.transpose(field, (0, 2, 1))


def shards(grid, quad_weights, orders, legendre, mix_real, mix_imag, filter_gain):
    lat_dev, chan, lon_count = grid.shape
    m_dev = legendre.shape[0]
    n_wide = lax.axis_size("wide")
    rest = lat_dev - SUB
    fits = (
        lax.axis_size("narrow") == 2
        and chan == LANES
        and lon_count % 96 == 0
        and m_dev == 2
        and 2 * rest == SUB
        and lat_dev % 2 == 0
        and n_wide % 16 == 0
        and n_wide & (n_wide - 1) == 0
        and lon_count * lon_count < 2**24
    )
    body = fast_shards if fits else general_shards
    return body(grid, quad_weights, orders, legendre, mix_real, mix_imag, filter_gain)


def solution(mesh):
    placed = (P("wide", "narrow", None), P("wide"), P(), P("wide", None, None), P(), P(), P())
    return jax.shard_map(
        shards, mesh=mesh, in_specs=placed, out_specs=P("wide", "narrow", None), check_vma=False
    )
```

```python
import functools
import math

import jax
import jax.numpy as jnp
from jax import lax
from jax.experimental import pallas as pl
from jax.experimental.pallas import tpu as pltpu
from jax.sharding import PartitionSpec as P

MESH = pl.DeviceIdType.MESH
SUB = 8
LANES = 128


def fourier_tables(orders, lon_count):
    columns = jnp.arange(lon_count, dtype=jnp.int32)
    phase_int = orders[:, None] * columns[None, :] % lon_count
    angles = phase_int.astype(jnp.float32) * (2.0 * math.pi / lon_count)
    return (jnp.cos(angles).astype(jnp.bfloat16), jnp.sin(angles).astype(jnp.bfloat16))


def general_shards(grid, quad_weights, orders, legendre, mix_real, mix_imag, filter_gain):
    lon_count = grid.shape[2]
    order_count = orders.shape[0]
    cosine_table, sine_table = fourier_tables(orders, lon_count)
    factor = 1.0 / math.sqrt(lon_count)
    real_part = (
        jnp.einsum("acn,kn->kac", grid, cosine_table, preferred_element_type=jnp.float32) * factor
    )
    imag_part = (
        -jnp.einsum("acn,kn->kac", grid, sine_table, preferred_element_type=jnp.float32) * factor
    )
    spectra = (
        jnp.stack([real_part, imag_part], axis=2) * quad_weights[None, :, None, None]
    ).astype(jnp.bfloat16)
    by_order = lax.all_to_all(spectra, "wide", split_axis=0, concat_axis=1, tiled=True)
    m_dev = by_order.shape[0]
    lat_count = by_order.shape[1]
    chan_dev = by_order.shape[3]
    deg_count = legendre.shape[1]
    coeffs = jnp.einsum(
        "mlx,mxk->mlk",
        legendre,
        by_order.reshape(m_dev, lat_count, 2 * chan_dev),
        preferred_element_type=jnp.float32,
    )
    coeffs = coeffs.astype(jnp.bfloat16).reshape(m_dev, deg_count, 2, chan_dev)
    deg_dev = deg_count // lax.axis_size("narrow")
    gain_rows = lax.dynamic_slice_in_dim(
        filter_gain, lax.axis_index("narrow") * deg_dev, deg_dev, 0
    ).astype(jnp.float32)
    upper = jnp.concatenate([mix_real, mix_imag], axis=1)
    lower = jnp.concatenate([-mix_imag, mix_real], axis=1)
    wide_block = jnp.concatenate([upper, lower], axis=0)
    fragment = lax.all_to_all(coeffs, "narrow", split_axis=1, concat_axis=3, tiled=True)
    frag_count = fragment.shape[0]
    chan_all = fragment.shape[3]
    flat_rows = fragment.reshape(frag_count * deg_dev, 2 * chan_all)
    product = jnp.dot(flat_rows, wide_block, preferred_element_type=jnp.float32)
    product = product.reshape(frag_count, deg_dev, 2, chan_all) * gain_rows[None, :, None, :]
    mixed_coeffs = product.astype(jnp.bfloat16)
    back_coeffs = lax.all_to_all(mixed_coeffs, "narrow", split_axis=3, concat_axis=1, tiled=True)
    synthesis = jnp.einsum(
        "mlx,mlk->mxk",
        legendre,
        back_coeffs.reshape(m_dev, deg_count, 2 * chan_dev),
        preferred_element_type=jnp.float32,
    )
    synthesis = synthesis.astype(jnp.bfloat16).reshape(m_dev, lat_count, 2, chan_dev)
    by_latitude = lax.all_to_all(synthesis, "wide", split_axis=1, concat_axis=0, tiled=True)
    field_out = jnp.einsum(
        "kac,kn->acn", by_latitude[:, :, 0], cosine_table, preferred_element_type=jnp.float32
    )
    field_out = field_out - jnp.einsum(
        "kac,kn->acn", by_latitude[:, :, 1], sine_table, preferred_element_type=jnp.float32
    )
    return (field_out / math.sqrt(order_count)).astype(jnp.bfloat16)


def turn_both(phase, period):
    quarter = period // 4
    turns = jnp.floor(phase * (1.0 / quarter) + 0.5)
    angle = (phase - turns * quarter) * (2.0 * math.pi / period)
    quadrant = turns - 4.0 * jnp.floor(turns * 0.25)
    sq = angle * angle
    cosine = 1.0 + sq * (-0.5 + sq * (1.0 / 24 + sq * (-1.0 / 720 + sq * (1.0 / 40320))))
    sine = angle * (1.0 + sq * (-1.0 / 6 + sq * (1.0 / 120 + sq * (-1.0 / 5040 + sq * (1.0 / 362880)))))
    odd = (quadrant == 1.0) | (quadrant == 3.0)
    first = jnp.where(odd, sine, cosine)
    second = jnp.where(odd, cosine, sine)
    first = jnp.where((quadrant == 1.0) | (quadrant == 2.0), -first, first)
    second = jnp.where(quadrant >= 2.0, -second, second)
    return first, second


def rotate(pair, by):
    return pair[0] * by[0] - pair[1] * by[1], pair[1] * by[0] + pair[0] * by[1]


def spectral_kernel(
    dims, orders_hbm, quad_hbm, grid_hbm, leg_hbm, mixr_hbm, mixi_hbm, gain_hbm,
    out_ref, tabt_ref,
    grid_v, leg_v, mixr_v, mixi_v, gain_v, tab, spread, send1, recv1, lt, lf,
    weight, blend, mixed, send2, recv2, flat2, orders_ref, quad_ref,
    grid_sem, in_sem, local_sem, s_send, s_recv, b_send, b_recv, ready,
):
    n_wide, lat_dev, lon_count, chan, m_dev, deg_count = dims
    order_count = n_wide * m_dev
    rows = 2 * order_count
    rest = lat_dev - SUB
    hw = n_wide // 2
    hs = hw * SUB
    pairs = lat_dev // 2
    others = m_dev * n_wide - 1
    me = lax.axis_index("wide")
    x = lax.axis_index("narrow")

    steps = []
    bit = 1
    while bit < n_wide:
        steps.append(bit * (1 - 2 * (me // bit % 2)))
        bit *= 2

    def flipped(d):
        return me + functools.reduce(
            lambda a, b: a + b, [s for i, s in enumerate(steps) if d >> i & 1], 0
        )

    partner = 1 - x
    across = [(flipped(d), partner) for d in reversed(range(n_wide))]
    along = [(flipped(d), x) for d in reversed(range(1, n_wide))]

    scalar_copies = []
    for i, (src, dst) in enumerate(((orders_hbm, orders_ref), (quad_hbm, quad_ref))):
        copy = pltpu.make_async_copy(src, dst, in_sem.at[4 + i])
        copy.start()
        scalar_copies.append(copy)
    grid_copies = []
    for p in range(pairs):
        copy = pltpu.make_async_copy(
            grid_hbm.at[pl.ds(2 * p, 2)], grid_v.at[pl.ds(2 * p, 2)], grid_sem.at[p]
        )
        copy.start()
        grid_copies.append(copy)

    late_low = n_wide - n_wide // 4
    late = me >= late_low
    barrier = pltpu.get_barrier_semaphore()

    @pl.when(jnp.logical_not(late))
    def _():
        for d in range(n_wide):
            for to in across[d:d + 1] + along[d:d + 1]:
                pl.semaphore_signal(barrier, inc=1, device_id=to, device_id_type=MESH)

    @pl.when(late)
    def _():
        for d in reversed(range(n_wide // 4)):
            for to in (flipped(d), partner), (flipped(d), x):
                if d or to[1] is partner:
                    pl.semaphore_signal(barrier, inc=1, device_id=to, device_id_type=MESH)

    for copy in scalar_copies:
        copy.wait()
    block_rows = 2 * n_wide
    sub = lax.broadcasted_iota(jnp.int32, (SUB, LANES), 0)
    pieces = []
    for j in range(m_dev):
        for low in range(0, n_wide, SUB):
            piece = jnp.zeros((SUB, LANES), jnp.int32)
            for i in range(SUB):
                piece = jnp.where(sub == i, orders_ref[(low + i) * m_dev + j], piece)
            pieces.append(piece)
    order_row = jnp.concatenate(pieces, axis=0)
    lane = lax.broadcasted_iota(jnp.int32, (order_count, LANES), 1)
    group = 4
    block = turn_both((order_row * lane).astype(jnp.float32), lon_count)
    one = turn_both((order_row * LANES).astype(jnp.float32), lon_count)
    far = turn_both((order_row * (group * LANES)).astype(jnp.float32), lon_count)
    for i, start in enumerate(range(0, lon_count, LANES)):
        size = min(LANES, lon_count - start)
        if i % group == 0:
            block = block if i == 0 else rotate(block, far)
            now = block
        else:
            now = rotate(now, one)
        for j in range(m_dev):
            here = slice(j * n_wide, (j + 1) * n_wide)
            top = j * block_rows
            tab[top:top + n_wide, start:start + size] = now[0][here, :size].astype(jnp.bfloat16)
            tab[top + n_wide:top + block_rows, start:start + size] = (
                -now[1][here, :size]
            ).astype(jnp.bfloat16)

    @pl.when(late)
    def _():
        pl.semaphore_wait(barrier, others)
        for w in range(3):
            pl.semaphore_signal(
                ready, inc=1, device_id=(w * (n_wide // 4) + me % (n_wide // 4), x),
                device_id_type=MESH,
            )

    factor = 1.0 / math.sqrt(lon_count)

    def transform(p):
        grid_copies[p].wait()
        rhs = jnp.concatenate([grid_v[2 * p], grid_v[2 * p + 1]], axis=1)
        res = jnp.dot(tab[...], rhs, preferred_element_type=jnp.float32)
        for i in range(2):
            a = 2 * p + i
            spread[a * rows:(a + 1) * rows, :] = res[:, i * chan:(i + 1) * chan] * (
                quad_ref[a] * factor
            )

    def row_of(j, ri, w):
        return j * block_rows + ri * n_wide + w

    whole, heads, tails = pl.ds(0, 3), pl.ds(0, 2), pl.ds(2, 1)

    def out_copy(part, to, where):
        return pltpu.make_async_remote_copy(
            src_ref=send1.at[to[1] * n_wide + to[0], where],
            dst_ref=recv1.at[x * n_wide + me, where],
            send_sem=s_send.at[part],
            recv_sem=s_recv.at[part],
            device_id=to,
            device_id_type=MESH,
        )

    mine = x * n_wide + me
    own_copy = pltpu.make_async_copy(send1.at[mine], recv1.at[mine], local_sem.at[0])

    def rearranged(a, count, j, w):
        first = a * rows
        return jnp.concatenate(
            [
                spread[pl.ds(first + row_of(j, ri, w), count, stride=rows), :]
                for ri in range(2)
            ],
            axis=0,
        ).astype(jnp.bfloat16)

    chunk = n_wide // 4
    lower = (me < n_wide // 2).astype(jnp.int32)

    first = 2

    def send_first(where):
        for w in range(first):
            @pl.when((w != me) | (x > 0))
            def _():
                out_copy(1 - lower, (w, 0), where).start()

    def send_quarter(q, where):
        part = 1 - lower if q < 2 else lower
        for i, side in enumerate((x, partner)):
            for w in reversed(range(q * chunk, (q + 1) * chunk)):
                wanted = (w != me) | (i > 0)
                if w < first:
                    wanted = wanted & (side > 0)

                @pl.when(wanted)
                def _():
                    out_copy(part, (w, side), where).start()

    def send_quarters(order, where):
        send_first(where)
        for q in order:
            send_quarter(q, where)

    for p in range(SUB // 2):
        transform(p)
    for j in range(m_dev):
        for w in range(n_wide):
            send1[j * n_wide + w, :2] = rearranged(0, SUB, j, w).reshape(2, SUB, chan)
    upper_half = me >= n_wide // 2

    @pl.when(upper_half)
    def _():
        @pl.when(late)
        def _():
            send_quarters((3, 2, 1, 0), heads)

        @pl.when(jnp.logical_not(late))
        def _():
            pl.semaphore_wait(barrier, 2 * late_low - 1)
            send_quarters((0, 1, 2), heads)

    for p in range(SUB // 2, pairs):
        transform(p)
    for j in range(m_dev):
        for w in range(n_wide):
            send1[j * n_wide + w, 2] = rearranged(SUB, rest, j, w)
    in_copies = []
    for i, (src, dst) in enumerate(
        ((leg_hbm.at[x], leg_v), (mixr_hbm, mixr_v), (mixi_hbm, mixi_v), (gain_hbm, gain_v))
    ):
        copy = pltpu.make_async_copy(src, dst, in_sem.at[i])
        copy.start()
        in_copies.append(copy)
    own_copy.start()

    @pl.when(upper_half)
    def _():
        @pl.when(late)
        def _():
            send_quarters((3, 2, 1, 0), tails)

        @pl.when(jnp.logical_not(late))
        def _():
            send_quarters((0, 1, 2), tails)

    @pl.when(jnp.logical_not(upper_half))
    def _():
        pl.semaphore_wait(barrier, 2 * late_low - 1)
        send_quarters((2, 1, 0), whole)

    @pl.when(jnp.logical_not(late))
    def _():
        pl.semaphore_wait(ready, 1)
        send_quarter(3, whole)

    for start in range(0, lon_count, LANES):
        size = min(LANES, lon_count - start)
        tabt_ref[start:start + size, :] = jnp.transpose(
            tab[:, start:start + size].astype(jnp.float32)
        ).astype(jnp.bfloat16)
    for copy in in_copies:
        copy.wait()
    lat_count = n_wide * lat_dev
    slot = lax.broadcasted_iota(jnp.int32, (4 * hs, lat_count), 0)
    lat = lax.broadcasted_iota(jnp.int32, (4 * hs, lat_count), 1)
    local = slot % SUB
    device = slot // (2 * hs) * hw + slot % hs // SUB
    head = slot % (2 * hs) < hs
    want = device * lat_dev + jnp.where(head, local, SUB + local % rest)
    pick = (want == lat).astype(jnp.bfloat16)
    moved = jnp.dot(pick, leg_v[...], preferred_element_type=jnp.float32)
    lt[...] = moved.astype(jnp.bfloat16)
    lf[...] = jnp.transpose(moved).astype(jnp.bfloat16)
    for i in range(m_dev):
        in_rows = slice(i * chan, (i + 1) * chan)
        for o in range(m_dev):
            re = mixr_v[in_rows, o * chan:(o + 1) * chan]
            im = mixi_v[in_rows, o * chan:(o + 1) * chan]
            top, left = 2 * i * chan, 2 * o * chan
            weight[top:top + chan, left:left + chan] = re
            weight[top:top + chan, left + chan:left + 2 * chan] = im
            weight[top + chan:top + 2 * chan, left:left + chan] = -im
            weight[top + chan:top + 2 * chan, left + chan:left + 2 * chan] = re

    def all_arrived(buf, count, sem):
        piece = buf.at[pl.ds(0, count)]
        pltpu.make_async_copy(piece, piece, sem).wait()

    tail_row = lax.broadcasted_iota(jnp.int32, (hs, chan), 0) % SUB
    upper = tail_row < rest

    def spectra_from(h):
        heads_of, tails_of = [], []
        for i in range(m_dev):
            there = pl.ds(i * n_wide + h * hw, hw)
            tail = recv1[there, 2].reshape(hs, chan)
            for ri in range(2):
                heads_of.append(recv1[there, ri].reshape(hs, chan))
                keep = upper if ri == 0 else jnp.logical_not(upper)
                tails_of.append(jnp.where(keep, tail, jnp.zeros_like(tail)))
        return jnp.concatenate(
            [jnp.concatenate(heads_of, axis=1), jnp.concatenate(tails_of, axis=1)], axis=0
        )

    def rows_from(h):
        return pl.ds(pl.multiple_of(h * 2 * hs, 2 * hs), 2 * hs)

    here, there = 1 - lower, lower
    own_copy.wait()
    all_arrived(recv1, n_wide - 1, s_recv.at[0])
    blend[rows_from(here), :] = jnp.dot(
        spectra_from(here), weight[...], preferred_element_type=jnp.float32
    ).astype(jnp.bfloat16)
    all_arrived(recv1, n_wide, s_recv.at[1])
    spec = spectra_from(there)

    def back_copy(to):
        return pltpu.make_async_remote_copy(
            src_ref=send2.at[to[1] * n_wide + to[0]],
            dst_ref=recv2.at[x * n_wide + me],
            send_sem=b_send,
            recv_sem=b_recv.at[x],
            device_id=to,
            device_id_type=MESH,
        )

    lead = range(first)
    order = [[(w, 0) for w in lead], [(w, 1) for w in lead]]
    for low in range(0, n_wide, chunk):
        for side in (0, 1):
            order[1] += [(w, side) for w in range(low, low + chunk) if w >= first]
    blend[rows_from(there), :] = jnp.dot(
        spec, weight[...], preferred_element_type=jnp.float32
    ).astype(jnp.bfloat16)
    step = deg_count // 1
    for low in range(0, deg_count, step):
        part = slice(low, low + step)
        product = jnp.dot(lf[part], blend[...], preferred_element_type=jnp.float32)
        gain = gain_v[part].astype(jnp.float32)
        gain = jnp.concatenate(
            [gain[:, o * chan:(o + 1) * chan] for o in range(m_dev) for _ in range(2)], axis=1
        )
        mixed[part] = (product * gain).astype(jnp.bfloat16)
    for o in range(m_dev):
        syn = jnp.dot(
            lt[...], mixed[:, 2 * o * chan:2 * (o + 1) * chan],
            preferred_element_type=jnp.float32,
        )
        for h in range(2):
            block = syn[h * 2 * hs:(h + 1) * 2 * hs]
            re, im = block[:, :chan], block[:, chan:]
            tail = jnp.where(upper, re[hs:], im[hs:])
            for t, tile in enumerate((re[:hs], im[:hs], tail)):
                send2[pl.ds(o * n_wide + h * hw, hw), t] = tile.astype(jnp.bfloat16).reshape(
                    hw, SUB, chan
                )
    for w, side in order[0] + order[1]:
        @pl.when((w != me) | (side != x))
        def _():
            back_copy((w, side)).start()

    mine = x * n_wide + me
    own_back = pltpu.make_async_copy(send2.at[mine], recv2.at[mine], local_sem.at[1])
    own_back.start()
    all_arrived(send1, n_wide - 1, s_send.at[0])
    all_arrived(send1, n_wide, s_send.at[1])
    own_back.wait()
    for who in (x, partner):
        all_arrived(recv2, n_wide - 1 if who is x else n_wide, b_recv.at[who])
        flat2[...] = recv2[pl.ds(who * n_wide, n_wide)].astype(jnp.float32).reshape(
            n_wide * 3 * SUB, chan
        )
        for a in range(lat_dev):
            for ri in range(2):
                at = ri * SUB + a if a < SUB else 2 * SUB + ri * rest + a - SUB
                top = pl.multiple_of(row_of(who, ri, 0), n_wide)
                out_ref[a, pl.ds(top, n_wide), :] = flat2[
                    pl.ds(at, n_wide, stride=3 * SUB), :
                ].astype(jnp.bfloat16)
    all_arrived(send2, others, b_send)


def field_kernel(scale, tile, tabt_ref, syn_ref, out_hbm, held, sem):
    lat_dev, lon_count, chan = held.shape
    copies = []
    for a in range(0, lat_dev, 2):
        rhs = jnp.concatenate([syn_ref[a], syn_ref[a + 1]], axis=1)
        for i, start in enumerate(range(0, lon_count, tile)):
            here = slice(start, start + tile)
            res = jnp.dot(tabt_ref[here], rhs, preferred_element_type=jnp.float32) * scale
            res = res.astype(jnp.bfloat16)
            held[a, here] = res[:, :chan]
            held[a + 1, here] = res[:, chan:]
            if i % 2:
                done = (pl.ds(a, 2), pl.ds(start - tile, 2 * tile))
                copy = pltpu.make_async_copy(
                    held.at[done], out_hbm.at[done], sem.at[len(copies)]
                )
                copy.start()
                copies.append(copy)
    for copy in copies:
        copy.wait()


def fast_shards(grid, quad_weights, orders, legendre, mix_real, mix_imag, filter_gain):
    lat_dev, chan, lon_count = grid.shape
    order_count = orders.shape[0]
    m_dev, deg_count, lat_count = legendre.shape
    n_wide = lax.axis_size("wide")
    rows = 2 * order_count
    half = n_wide * SUB
    bf16, f32 = jnp.bfloat16, jnp.float32
    vmem = pl.BlockSpec(memory_space=pltpu.VMEM)
    hbm = pl.BlockSpec(memory_space=pltpu.HBM)
    dims = (n_wide, lat_dev, lon_count, chan, m_dev, deg_count)
    chan_all = mix_real.shape[0]
    dma = pltpu.SemaphoreType.DMA
    synthesis, table = pl.pallas_call(
        functools.partial(spectral_kernel, dims),
        out_shape=(
            jax.ShapeDtypeStruct((lat_dev, rows, chan), bf16),
            jax.ShapeDtypeStruct((lon_count, rows), bf16),
        ),
        in_specs=[hbm] * 7,
        out_specs=(vmem, vmem),
        scratch_shapes=[
            pltpu.VMEM((lat_dev, lon_count, chan), bf16),
            pltpu.VMEM((lat_count, deg_count), bf16),
            pltpu.VMEM((chan_all, chan_all), bf16),
            pltpu.VMEM((chan_all, chan_all), bf16),
            pltpu.VMEM((deg_count, chan_all), bf16),
            pltpu.VMEM((rows, lon_count), bf16),
            pltpu.VMEM((lat_dev * rows, chan), f32),
            pltpu.VMEM((order_count, 3, SUB, chan), bf16),
            pltpu.VMEM((order_count, 3, SUB, chan), bf16),
            pltpu.VMEM((2 * half, deg_count), bf16),
            pltpu.VMEM((deg_count, 2 * half), bf16),
            pltpu.VMEM((4 * chan, 4 * chan), bf16),
            pltpu.VMEM((2 * half, 4 * chan), bf16),
            pltpu.VMEM((deg_count, 4 * chan), bf16),
            pltpu.VMEM((order_count, 3, SUB, chan), bf16),
            pltpu.VMEM((order_count, 3, SUB, chan), bf16),
            pltpu.VMEM((n_wide * 3 * SUB, chan), f32),
            pltpu.SMEM((order_count,), jnp.int32),
            pltpu.SMEM((lat_dev,), f32),
            dma((lat_dev // 2,)),
            dma((6,)),
            dma((2,)),
            dma((2,)),
            dma((2,)),
            dma,
            dma((2,)),
            pltpu.SemaphoreType.REGULAR,
        ],
        compiler_params=pltpu.CompilerParams(
            collective_id=0, has_side_effects=True, vmem_limit_bytes=40 * 2**20
        ),
        name="spectral",
    )(*(pltpu.with_memory_space_constraint(v, pltpu.HBM) for v in (
        orders, quad_weights, jnp.transpose(grid, (0, 2, 1)), jnp.transpose(legendre, (0, 2, 1)),
        mix_real, mix_imag, filter_gain,
    )))
    field = pl.pallas_call(
        functools.partial(field_kernel, 1.0 / math.sqrt(order_count), lon_count // 6),
        out_shape=jax.ShapeDtypeStruct((lat_dev, lon_count, chan), bf16),
        in_specs=[vmem, vmem],
        out_specs=pl.BlockSpec(memory_space=pl.ANY),
        scratch_shapes=[pltpu.VMEM((lat_dev, lon_count, chan), bf16), dma((3 * lat_dev // 2,))],
        compiler_params=pltpu.CompilerParams(vmem_limit_bytes=24 * 2**20),
        name="field",
    )(table, synthesis)
    return jnp.transpose(field, (0, 2, 1))


def shards(grid, quad_weights, orders, legendre, mix_real, mix_imag, filter_gain):
    lat_dev, chan, lon_count = grid.shape
    m_dev = legendre.shape[0]
    n_wide = lax.axis_size("wide")
    rest = lat_dev - SUB
    fits = (
        lax.axis_size("narrow") == 2
        and chan == LANES
        and lon_count % 96 == 0
        and m_dev == 2
        and 2 * rest == SUB
        and lat_dev % 2 == 0
        and n_wide % 16 == 0
        and n_wide & (n_wide - 1) == 0
        and lon_count * lon_count < 2**24
    )
    body = fast_shards if fits else general_shards
    return body(grid, quad_weights, orders, legendre, mix_real, mix_imag, filter_gain)


def solution(mesh):
    placed = (P("wide", "narrow", None), P("wide"), P(), P("wide", None, None), P(), P(), P())
    return jax.shard_map(
        shards, mesh=mesh, in_specs=placed, out_specs=P("wide", "narrow", None), check_vma=False
    )
```
